128 devices in a mesh: angle: 8 (over x_hi, y), row: 16 (over z, x_lo, core).
Axes of the slice: x: 4 (x_hi: 2, x_lo: 2; x = x_hi * 2 + x_lo), y: 4, z: 4, core: 2. Of those that a mesh axis runs over, the one named last changes fastest.
Arguments:
- intensity: float32 [1024, 16, 4096], P('angle', 'row'), may hold values from 0.036 to 1
- flat_field: float32 [16, 4096], P('row'), may hold values from 1 to 2
- dark_field: float32 [16, 4096], P('row'), may hold values from 0 to 0.02
- correlation: int32 [1], replicated, may hold values from 512 to 1536
- blend_width: int32 [1], replicated, may hold values from 64 to 511
- padding: int32 [1], replicated, may hold values from 1024 to 4096
- cutoff: int32 [1], replicated, may hold values from 1 to 8
Outputs:
- sinogram: float32 [512, 16, 8192], P('angle', 'row')
The draws below stay inside these ranges and needn't reach their ends.
All inputs are finite; a program needn't handle non-finite values.
Results may differ from the reference program's by a relative error of at most 0.00023.
Values sent between devices are 32-bit elements; how exact they have to be, the bound alone decides.
A program may use at most 128 MiB of HBM per device.

```python
import math
import jax
import jax.numpy as jnp
from jax import lax

DET = 4096
HB = 64
KMAX = 8
HALF = 512
ANGLES = 1024
ROWS = 16
FCUT = 512
OVL_LO = 512
OVL_HI = 1536
BLEND_LO = 64
BLEND_HI = 511
PAD_LO = 1024
PAD_HI = 4096
N_ANGLE = 8


def draw_intensity(key, part):
    noise_key, amp_key, phase_key = jax.random.split(key, 3)
    full_shape = (ANGLES, ROWS, DET)
    noise_factor = jax.random.uniform(noise_key, full_shape, jnp.float32, 0.4, 1.0)
    amplitude = jax.random.uniform(amp_key, (8, ROWS, DET), jnp.float32, 0.0, 0.15)
    phase_shift = jax.random.uniform(phase_key, (8, ROWS, DET), jnp.float32, -math.pi, math.pi)
    angle_index = jnp.arange(ANGLES, dtype=jnp.int32)
    exponent = jnp.zeros(full_shape, jnp.float32)
    for harmonic in range(1, 9):
        turn_angle = (harmonic * angle_index % HALF).astype(jnp.float32) * (2.0 * math.pi / HALF)
        exponent = exponent + amplitude[harmonic - 1] * (1.0 + jnp.cos(turn_angle[:, None, None] + phase_shift[harmonic - 1]))
    return noise_factor * jnp.exp(-exponent)


def levels(own_key, dims, shards, least, largest):
    loudness, own = 1.0, jax.random.fold_in(own_key, 6)
    for dim, parts in shards:
        steps = jnp.exp(jax.random.uniform(jax.random.fold_in(own, dim), (parts,), jnp.float32, least / len(shards), largest / len(shards)))
        loudness = loudness * jnp.repeat(steps, dims[dim] // parts).reshape([-1 if axis == dim else 1 for axis in range(len(dims))])
    return loudness


def setup_inputs(seed: int = 0) -> dict:
    arg_keys = jax.random.split(jax.random.key(seed), 8)
    return {
        "intensity": draw_intensity(jax.random.fold_in(arg_keys[7], 71), 0),
        "flat_field": jnp.clip(1.0 + 1.0 * jax.random.uniform(arg_keys[1], (ROWS, DET), jnp.float32) ** levels(arg_keys[1], (ROWS, DET), ((0, 16),), -0.2, 0.2), 1.0, 2.0),
        "dark_field": jnp.clip(0.02 * jax.random.uniform(arg_keys[2], (ROWS, DET), jnp.float32) ** levels(arg_keys[2], (ROWS, DET), ((0, 16),), -0.2, 0.2), 0.0, 0.02),
        "correlation": jax.random.randint(arg_keys[3], (1,), OVL_LO, OVL_HI + 1).astype(jnp.int32),
        "blend_width": jax.random.randint(arg_keys[4], (1,), BLEND_LO, BLEND_HI + 1).astype(jnp.int32),
        "padding": jax.random.randint(arg_keys[5], (1,), PAD_LO, PAD_HI + 1).astype(jnp.int32),
        "cutoff": jax.random.randint(arg_keys[6], (1,), 1, KMAX + 1).astype(jnp.int32),
    }


def stitch(main_view, back_view, correlation, blend_size):
    pixels = main_view.shape[-1]
    leading = main_view.shape[:-1]
    last_axis = main_view.ndim - 1
    empty = jnp.zeros(leading + (pixels,), main_view.dtype)
    edge_hold = jnp.broadcast_to(main_view[..., -1:], leading + (pixels,))
    extended_main = jnp.concatenate([empty, main_view, edge_hold], axis=-1)
    right_side = lax.dynamic_slice_in_dim(extended_main, correlation, 2 * pixels, last_axis)
    left_side = jnp.concatenate([jnp.flip(back_view, -1), empty], axis=-1)
    position = jnp.arange(2 * pixels).astype(main_view.dtype)
    center = pixels - correlation.astype(main_view.dtype) / 2.0
    weight_right = jnp.clip((position + 0.5 - center) / blend_size.astype(main_view.dtype) + 0.5, 0.0, 1.0)
    return left_side * (1.0 - weight_right) + right_side * weight_right


def extend(stitched, padding, length):
    width_now = stitched.shape[-1]
    leading = stitched.shape[:-1]
    base_row = jnp.concatenate([stitched, jnp.zeros(leading + (length - width_now,), stitched.dtype)], axis=-1)
    index_list = jnp.arange(length, dtype=jnp.int32)
    right_mask = (index_list >= width_now) & (index_list < width_now + padding)
    left_mask = index_list >= length - padding
    return base_row + jnp.where(right_mask, stitched[..., -1:], 0.0) + jnp.where(left_mask, stitched[..., :1], 0.0)


def reference(intensity, flat_field, dark_field, correlation, blend_width, padding, cutoff):
    shift_by = correlation[0]
    blend_size = blend_width[0]
    margin = padding[0]
    limit_order = cutoff[0]
    projected = -jnp.log((intensity - dark_field) / (flat_field - dark_field))
    by_row = jnp.transpose(projected, (1, 0, 2))
    length = 4 * DET
    kept_bins = 2 * DET
    frequency = jnp.arange(kept_bins).astype(jnp.float32)
    ramp_gain = (frequency / kept_bins) * (1.0 + jnp.cos(math.pi * frequency / kept_bins))
    drop_gain = 1.0 - 1.0 / (1.0 + (frequency / FCUT) ** 8)
    orders = jnp.arange(HALF, dtype=jnp.int32)
    chosen = ((orders < limit_order) | (orders > HALF - limit_order)).astype(jnp.float32)[:, None]

    def one_row(sheet):
        stitched = stitch(sheet[:HALF], sheet[HALF:], shift_by, blend_size)
        extended = extend(stitched, margin, length)
        spectrum = jnp.fft.fft(extended, axis=-1)[:, :kept_bins]
        low_part = jnp.fft.ifft(jnp.fft.fft(spectrum, axis=0) * chosen, axis=0)
        filtered = (spectrum - drop_gain * low_part) * ramp_gain
        padded_spec = jnp.concatenate([filtered, jnp.zeros((HALF, 1), filtered.dtype)], axis=1)
        return jnp.fft.irfft(padded_spec, n=length, axis=-1)[:, :kept_bins]

    cleaned = lax.map(one_row, by_row)
    order_index = jnp.arange(HALF, dtype=jnp.int32)
    block_index = order_index // HB
    inner_index = order_index % HB
    halves = N_ANGLE // 2
    source = (block_index % halves) * 2 * HB + (block_index // halves) * HB + inner_index
    return jnp.transpose(cleaned, (1, 0, 2))[source].astype(jnp.float32)
```

```python
import functools
import math

import jax
import jax.numpy as jnp
import numpy as np
from jax import lax
from jax.experimental import pallas as pl
from jax.experimental.pallas import tpu as pltpu
from jax.sharding import PartitionSpec as P

KMAX = 8
FCUT = 512
LANE = 128
MODES = 16
CHUNK = 8
STACK = 80


def split_np(table):
    high = table.astype(jnp.bfloat16)
    low = (table - high.astype(np.float64)).astype(jnp.bfloat16)
    return high, low


def split(value):
    high = value.astype(jnp.bfloat16)
    low = (value - high.astype(jnp.float32)).astype(jnp.bfloat16)
    return high, low


def split_outside(value):
    high = lax.reduce_precision(value, 8, 7)
    return high.astype(jnp.bfloat16), (value - high).astype(jnp.bfloat16)


@functools.cache
def constants(length):
    kept = length // 2
    freq = np.arange(kept, dtype=np.float64)
    ramp = freq / kept * (1.0 + np.cos(np.pi * freq / kept))
    drop = 1.0 - 1.0 / (1.0 + (freq / FCUT) ** 8)
    half = LANE // 2
    gains, sums = [], []
    reach = length * 3 // 4
    for gain in (ramp, ramp * drop):
        full = np.zeros(length)
        full[:kept] = gain
        full[kept + 1 :] = gain[:0:-1]
        kernel = np.fft.ifft(full).real
        offsets = np.arange(-reach, reach + 1)
        sums.append(np.concatenate([[0.0], np.cumsum(kernel[offsets % length])]))
        place = np.arange(length)
        signed = np.where(place < kept, place, place - length)
        turned = kernel * np.exp(-1j * np.pi * signed / length)
        turned[kept] = 0.0
        between = np.fft.fft(turned).real
        k1 = np.arange(half)[:, None]
        k2 = np.arange(LANE)[None, :]
        gains.append(between[k1 + LANE * k2] * (2.0 / length))
    k1 = np.arange(half)[:, None]
    n2 = np.arange(LANE)[None, :]
    turn = 2.0 * np.pi * (k1 + 0.5) * n2 / length
    twiddle = np.stack([np.cos(turn), np.sin(turn)]).astype(np.float32)
    a = np.arange(LANE)[:, None]
    b = np.arange(LANE)[None, :]
    angle = 2.0 * np.pi * (a * b % LANE) / LANE
    c, s = np.cos(angle), np.sin(angle)
    forward = split_np(np.block([[c, -s], [s, c]]))
    backward = split_np(np.block([[c, s], [-s, c]]))
    n1 = np.arange(half)[:, None]
    last = 2.0 * np.pi * ((2 * np.arange(half)[None, :] + 1) * n1 % (2 * LANE)) / (2 * LANE)
    high, low = split_np(np.concatenate([np.cos(last), -np.sin(last)], axis=1))
    final = np.concatenate([high, high, low], axis=1)
    return (
        np.stack(gains).astype(np.float32),
        np.stack(sums).astype(np.float32),
        twiddle,
        np.concatenate([forward[0], forward[1]], axis=0),
        np.concatenate([backward[0], backward[1]], axis=0),
        final,
        reach,
    )


def dot(a, b):
    return jnp.dot(a, b, preferred_element_type=jnp.float32)


def modes_kernel(x_ref, flat_ref, dark_ref, phi_ref, o_ref):
    count = phi_ref.shape[1] // 3
    blocks = flat_ref.shape[0]
    phi = phi_ref[...]
    for n1 in range(blocks):
        dark = dark_ref[n1 : n1 + 1, :]
        base = jnp.log(flat_ref[n1 : n1 + 1, :] - dark)
        rows = x_ref[pl.ds(n1, count, stride=blocks), :]
        high, low = split(base - jnp.log(rows - dark))
        o_ref[pl.ds(n1, MODES, stride=blocks), :] = dot(phi, jnp.concatenate([high, low, high], axis=0))


def modes(x, flat, dark, phi):
    blocks = flat.shape[0]
    return pl.pallas_call(
        modes_kernel,
        out_shape=jax.ShapeDtypeStruct((MODES * blocks, LANE), jnp.float32),
        in_specs=[pl.BlockSpec(memory_space=pltpu.VMEM)] * 4,
        out_specs=pl.BlockSpec(memory_space=pltpu.VMEM),
        compiler_params=pltpu.CompilerParams(vmem_limit_bytes=32 << 20),
        cost_estimate=pl.CostEstimate(flops=50000000, bytes_accessed=3000000, transcendentals=600000),
        name="modes",
    )(x, flat, dark, phi)


def main_kernel(
    s_ref,
    own_ref,
    got_ref,
    gm_ref,
    gb_ref,
    flat_ref,
    dark_ref,
    first_ref,
    coef_ref,
    edge_ref,
    gain_ref,
    tw_ref,
    fwd_ref,
    bwd_ref,
    fin_ref,
    out_ref,
    main_s,
    back_s,
    shift_s,
    yh_s,
    yl_s,
    res_s,
    bg_s,
    corr_s,
    edge_s,
):
    step = pl.program_id(0)
    mode_steps = MODES // CHUNK
    half = LANE // 2
    upper = s_ref[0]
    roll_by = s_ref[1]
    halfcorr = s_ref[2].astype(jnp.float32) * 0.5
    blend = s_ref[3].astype(jnp.float32)
    blocks = flat_ref.shape[0]

    is_mode = step < mode_steps

    @pl.when(is_mode)
    def _():
        main_s[...] = gm_ref[...]
        back_s[...] = gb_ref[...]

    @pl.when(jnp.logical_not(is_mode))
    def _():
        dark = dark_ref[...]
        base = jnp.log(flat_ref[...] - dark)
        own = base - jnp.log(own_ref[...] - dark)
        got = base - jnp.log(got_ref[...] - dark)
        main_s[...] = jnp.where(upper == 1, got, own)
        back_s[...] = jnp.where(upper == 1, own, got)

    @pl.when(step == 0)
    def _():
        shift_s[...] = jnp.zeros_like(shift_s)

    pixel = (
        lax.broadcasted_iota(jnp.int32, (blocks, LANE), 0) * LANE
        + lax.broadcasted_iota(jnp.int32, (blocks, LANE), 1)
    ).astype(jnp.float32)
    weight = jnp.clip((pixel + 0.5 - halfcorr) / blend + 0.5, 0.0, 1.0)
    lanes = lax.broadcasted_iota(jnp.int32, (blocks, LANE), 1)
    lanes48 = lax.broadcasted_iota(jnp.int32, (STACK - blocks, LANE), 1)
    tall = shift_s.shape[1]
    for t in range(0, CHUNK, 2):
        parts = []
        for i in (t, t + 1):
            main = main_s[i]
            back = back_s[i]
            edge_s[0, i : i + 1, :] = jnp.broadcast_to(main[blocks - 1 : blocks, LANE - 1 :], (1, LANE))
            edge_s[1, i : i + 1, :] = jnp.broadcast_to(back[blocks - 1 : blocks, LANE - 1 :], (1, LANE))
            left = jnp.take_along_axis(back * weight, LANE - 1 - lanes, axis=1)
            shift_s[i, 8 : 8 + blocks, :] = pltpu.roll(main * weight, roll_by, 1)
            here = shift_s[i, 8 : 8 + STACK - blocks, :]
            prev = shift_s[i, 7 : 7 + STACK - blocks, :]
            right = jnp.where(lanes48 >= roll_by, here, prev)
            parts.append(jnp.concatenate([left, right], axis=0))
        high, low = split(jnp.concatenate(parts, axis=1))
        y = dot(first_ref[...], jnp.concatenate([high, low, high], axis=0))
        cos, sin = tw_ref[0], tw_ref[1]
        for j, i in enumerate((t, t + 1)):
            re = y[:half, j * LANE : (j + 1) * LANE]
            im = y[half:, j * LANE : (j + 1) * LANE]
            turned = jnp.concatenate([re * cos + im * sin, im * cos - re * sin], axis=1)
            high, low = split(turned)
            yh_s[i * half : (i + 1) * half, :] = high
            yl_s[i * half : (i + 1) * half, :] = low
    wide = 2 * LANE
    which = is_mode.astype(jnp.int32)
    gain = gain_ref[which]
    gain2 = jnp.concatenate([gain, gain], axis=1)
    for t in range(0, CHUNK, 2):
        rows = slice(t * half, (t + 2) * half)
        z = (
            dot(yh_s[rows, :], fwd_ref[:wide, :])
            + dot(yl_s[rows, :], fwd_ref[:wide, :])
            + dot(yh_s[rows, :], fwd_ref[wide:, :])
        )
        z = z * jnp.concatenate([gain2, gain2], axis=0)
        high, low = split(z)
        u = dot(high, bwd_ref[:wide, :]) + dot(low, bwd_ref[:wide, :]) + dot(high, bwd_ref[wide:, :])
        parts = []
        cos, sin = tw_ref[0], tw_ref[1]
        for j in range(2):
            re = u[j * half : (j + 1) * half, :LANE]
            im = u[j * half : (j + 1) * half, LANE:]
            parts.append(jnp.concatenate([re * cos - im * sin, im * cos + re * sin], axis=0))
        high, low = split(jnp.concatenate(parts, axis=1))
        o = dot(fin_ref[...], jnp.concatenate([high, low, high], axis=0))
        for j in range(2):
            i = t + j
            res_s[i] = (
                o[:, j * LANE : (j + 1) * LANE]
                + edge_s[0, i : i + 1, :] * edge_ref[which, 0]
                + edge_s[1, i : i + 1, :] * edge_ref[which, 1]
            )

    @pl.when(is_mode)
    def _():
        for i in range(CHUNK):
            bg_s[pl.ds((step * CHUNK + i) * half, half), :] = res_s[i]

    @pl.when(step == mode_steps - 1)
    def _():
        count = coef_ref.shape[0]
        for n1 in range(half):
            high, low = split(bg_s[pl.ds(n1, MODES, stride=half), :])
            corr_s[pl.ds(n1, count, stride=half), :] = dot(
                coef_ref[...], jnp.concatenate([high, low, high], axis=0)
            )

    @pl.when(jnp.logical_not(is_mode))
    def _():
        for i in range(CHUNK):
            row = ((step - mode_steps) * CHUNK + i) * half
            out_ref[i] = res_s[i] + corr_s[pl.ds(row, half), :]


def filter_rows(scalars, own, got, gm, gb, flat, dark, first, coef, edge, gain, tw, fwd, bwd, fin):
    count = got.shape[0]
    blocks = flat.shape[0]
    half = LANE // 2
    mode_steps = MODES // CHUNK
    halves = count // CHUNK

    def whole(a):
        return pl.BlockSpec(a.shape, lambda i, s, n=a.ndim: (0,) * n)

    def rows(i, s):
        return (jnp.maximum(i - mode_steps, 0), 0, 0)

    grid_spec = pltpu.PrefetchScalarGridSpec(
        num_scalar_prefetch=1,
        grid=(mode_steps + halves,),
        in_specs=[
            pl.BlockSpec(
                (CHUNK, blocks, LANE), lambda i, s: (s[0] * halves + jnp.maximum(i - mode_steps, 0), 0, 0)
            ),
            pl.BlockSpec((CHUNK, blocks, LANE), rows),
            pl.BlockSpec((CHUNK, blocks, LANE), lambda i, s: (jnp.minimum(i, mode_steps - 1), 0, 0)),
            pl.BlockSpec((CHUNK, blocks, LANE), lambda i, s: (jnp.minimum(i, mode_steps - 1), 0, 0)),
            *[whole(a) for a in (flat, dark, first, coef, edge, gain, tw, fwd, bwd, fin)],
        ],
        out_specs=pl.BlockSpec((CHUNK, half, LANE), rows),
        scratch_shapes=[
            pltpu.VMEM((CHUNK, blocks, LANE), jnp.float32),
            pltpu.VMEM((CHUNK, blocks, LANE), jnp.float32),
            pltpu.VMEM((CHUNK, STACK - blocks + 8, LANE), jnp.float32),
            pltpu.VMEM((CHUNK * half, 2 * LANE), jnp.bfloat16),
            pltpu.VMEM((CHUNK * half, 2 * LANE), jnp.bfloat16),
            pltpu.VMEM((CHUNK, half, LANE), jnp.float32),
            pltpu.VMEM((MODES * half, LANE), jnp.float32),
            pltpu.VMEM((count * half, LANE), jnp.float32),
            pltpu.VMEM((2, CHUNK, LANE), jnp.float32),
        ],
    )
    return pl.pallas_call(
        main_kernel,
        out_shape=jax.ShapeDtypeStruct((count, half, LANE), jnp.float32),
        grid_spec=grid_spec,
        compiler_params=pltpu.CompilerParams(vmem_limit_bytes=40 << 20),
        cost_estimate=pl.CostEstimate(flops=10000000000, bytes_accessed=6000000, transcendentals=600000),
        name="filter_rows",
    )(scalars, own, got, gm, gb, flat, dark, first, coef, edge, gain, tw, fwd, bwd, fin)


def phase(orders, angles, half_turn):
    turn = (orders[:, None] * angles[None, :] % half_turn).astype(jnp.float32) * (2.0 * math.pi / half_turn)
    return jnp.concatenate([jnp.cos(turn), jnp.sin(turn)], axis=0)


def local(intensity, flat_field, dark_field, correlation, blend_width, padding, cutoff):
    angle_count = lax.axis_size("angle")
    place = lax.axis_index("angle")
    total = intensity.shape[0]
    half_block = total // 2
    pixels = intensity.shape[2]
    length = 4 * pixels
    blocks = pixels // LANE
    half = LANE // 2
    halves = angle_count // 2
    half_turn = half_block * angle_count
    upper = (place >= halves).astype(jnp.int32)
    gains, sums, tw, fwd, bwd, fin, reach = constants(length)

    x = intensity.reshape(total, blocks, LANE)
    flat = flat_field.reshape(blocks, LANE)
    dark = dark_field.reshape(blocks, LANE)
    outgoing = lax.dynamic_slice_in_dim(x, (1 - upper) * half_block, half_block, 0)
    pairs = [(source, source ^ halves) for source in range(angle_count)]
    got = lax.ppermute(outgoing, "angle", pairs)

    orders = jnp.arange(KMAX, dtype=jnp.int32)
    own_angles = place % halves * total + jnp.arange(total, dtype=jnp.int32)
    phi_high, phi_low = split_outside(phase(orders, own_angles, half_turn))
    mine = modes(
        x.reshape(total * blocks, LANE), flat, dark, jnp.concatenate([phi_high, phi_high, phi_low], axis=1)
    )
    slots = jnp.where(jnp.arange(2)[:, None, None] == upper, mine[None], 0.0)
    both = lax.psum(slots, "angle").reshape(2, MODES, blocks, LANE)

    shift = pixels - correlation[0]
    q, r = shift // LANE, shift % LANE
    k1 = jnp.arange(half, dtype=jnp.int32)[:, None]
    index = jnp.concatenate(
        [blocks - 1 - jnp.arange(blocks, dtype=jnp.int32), q + jnp.arange(STACK - blocks, dtype=jnp.int32)]
    )[None, :]
    turn = ((2 * k1 + 1) * index % (2 * LANE)).astype(jnp.float32) * (math.pi / LANE)
    high, low = split_outside(jnp.concatenate([jnp.cos(turn), -jnp.sin(turn)], axis=0))
    first = jnp.concatenate([high, high, low], axis=1)

    out_angles = place % halves * total + upper * half_block + jnp.arange(half_block, dtype=jnp.int32)
    scale = jnp.where(orders < cutoff[0], jnp.where(orders == 0, 1.0, 2.0), 0.0) * (-1.0 / half_turn)
    coef = (phase(orders, out_angles, half_turn) * jnp.concatenate([scale, scale])[:, None]).T
    high, low = split_outside(coef)
    coef = jnp.concatenate([high, high, low], axis=1)

    kept = 2 * pixels
    table = jnp.asarray(sums)

    def cut(start):
        return lax.dynamic_slice_in_dim(table, start + reach, kept, 1)

    tail = cut(1 - kept + correlation[0]) - cut(1 - kept - padding[0])
    head = cut(1 + padding[0]) - cut(1)
    edge = jnp.stack([tail, head], axis=1).reshape(2, 2, half, LANE)
    scalars = jnp.stack([upper, r, correlation[0], blend_width[0]])
    out = filter_rows(
        scalars, x, got, both[0], both[1], flat, dark, first, coef, edge,
        jnp.asarray(gains), jnp.asarray(tw), jnp.asarray(fwd), jnp.asarray(bwd), jnp.asarray(fin),
    )
    return out.reshape(half_block, 1, kept)


def solution(mesh):
    placed = (P("angle", "row", None), P("row", None), P("row", None), P(), P(), P(), P())
    return jax.shard_map(
        local, mesh=mesh, in_specs=placed, out_specs=P("angle", "row", None), check_vma=False
    )
```

```python
import functools

import jax
import jax.numpy as jnp
import numpy as np
from jax import lax
from jax.experimental import pallas as pl
from jax.experimental.pallas import tpu as pltpu
from jax.sharding import PartitionSpec as P

KMAX = 8
FCUT = 512
OVL_LO = 512
OVL_HI = 1536
LANE = 128
MODES = 16
GROUP = 4
CHUNK = 8
STACK = 80
MODE_STEP = 2
CORR_STEP = 6
MESH = pl.DeviceIdType.MESH


def split_np(table):
    high = table.astype(jnp.bfloat16)
    low = (table - high.astype(np.float64)).astype(jnp.bfloat16)
    return high, low


def split(value):
    high = value.astype(jnp.bfloat16)
    low = (value - high.astype(jnp.float32)).astype(jnp.bfloat16)
    return high, low


@functools.cache
def constants(length, angle_count, total):
    kept = length // 2
    freq = np.arange(kept, dtype=np.float64)
    ramp = freq / kept * (1.0 + np.cos(np.pi * freq / kept))
    drop = 1.0 - 1.0 / (1.0 + (freq / FCUT) ** 8)
    half = LANE // 2
    gains, sums = [], []
    reach = length * 3 // 4
    for gain in (ramp, ramp * drop):
        full = np.zeros(length)
        full[:kept] = gain
        full[kept + 1 :] = gain[:0:-1]
        kernel = np.fft.ifft(full).real
        offsets = np.arange(-reach, reach + 1)
        table = np.concatenate([[0.0], np.cumsum(kernel[offsets % length])])
        sums.append(np.pad(table, (0, -len(table) % LANE + LANE)).reshape(-1, LANE))
        place = np.arange(length)
        signed = np.where(place < kept, place, place - length)
        turned = kernel * np.exp(-1j * np.pi * signed / length)
        turned[kept] = 0.0
        between = np.fft.fft(turned).real
        k1 = np.arange(half)[:, None]
        k2 = np.arange(LANE)[None, :]
        gains.append(between[k1 + LANE * k2] * (2.0 / length))
    k1 = np.arange(half)[:, None]
    n2 = np.arange(LANE)[None, :]
    turn = 2.0 * np.pi * (k1 + 0.5) * n2 / length
    twiddle = np.stack([np.cos(turn), np.sin(turn)]).astype(np.float32)
    a = np.arange(LANE)[:, None]
    b = np.arange(LANE)[None, :]
    angle = 2.0 * np.pi * (a * b % LANE) / LANE
    c, s = np.cos(angle), np.sin(angle)
    forward = np.concatenate(split_np(np.block([[c, -s], [s, c]])), axis=0)
    backward = np.concatenate(split_np(np.block([[c, s], [-s, c]])), axis=0)
    n1 = np.arange(half)[:, None]
    last = 2.0 * np.pi * ((2 * np.arange(half)[None, :] + 1) * n1 % (2 * LANE)) / (2 * LANE)
    high, low = split_np(np.concatenate([np.cos(last), -np.sin(last)], axis=1))
    final = np.concatenate([high, high, low], axis=1)
    blocks = length // 4 // LANE
    firsts = []
    for q in range((length // 4 - OVL_HI) // LANE, (length // 4 - OVL_LO) // LANE + 1):
        index = np.concatenate([blocks - 1 - np.arange(blocks), q + np.arange(STACK - blocks)])[None, :]
        turn = np.pi * ((2 * k1 + 1) * index % (2 * LANE)) / LANE
        high, low = split_np(np.concatenate([np.cos(turn), -np.sin(turn)], axis=0))
        firsts.append(np.concatenate([high, high, low], axis=1))
    halves = angle_count // 2
    half_turn = angle_count * total // 2
    orders = np.arange(KMAX)[:, None]
    phis, coefs = [], []
    for place in range(angle_count):
        base = place % halves * total
        turn = 2.0 * np.pi * (orders * (base + np.arange(total)[None, :]) % half_turn) / half_turn
        table = np.concatenate([np.cos(turn), np.sin(turn)], axis=0)
        if place < halves:
            high, low = split_np(table)
            phis.append(np.concatenate([high, high, low], axis=1))
        start = place // halves * (total // 2)
        table = table[:, start : start + total // 2] * (-2.0 / half_turn)
        table[0] *= 0.5
        groups = table.reshape(halves, GROUP, -1)
        table = np.concatenate([groups[(place % halves - k) % halves] for k in range(halves)], axis=0)
        high, low = split_np(table.T)
        coefs.append(np.concatenate([high, high, low], axis=1))
    return dict(
        phi=np.concatenate(phis, axis=0),
        first=np.concatenate(firsts, axis=0),
        sums=np.concatenate(sums, axis=0).astype(np.float32),
        gain=np.concatenate(gains, axis=0).astype(np.float32),
        twiddle=twiddle.reshape(2 * half, LANE),
        forward=forward,
        backward=backward,
        final=final,
        coef=np.concatenate(coefs, axis=0),
    )


def dot(a, b):
    return jnp.dot(a, b, preferred_element_type=jnp.float32)


def cut(sums_s, which, start):
    half = LANE // 2
    rows = sums_s.shape[0] // 2
    row = lax.shift_right_logical(start, 7)
    rest = jnp.bitwise_and(start, LANE - 1)
    back = jnp.bitwise_and(LANE - rest, LANE - 1)
    here = pltpu.roll(sums_s[pl.ds(which * rows + row, half), :], back, 1)
    there = pltpu.roll(sums_s[pl.ds(which * rows + row + 1, half), :], back, 1)
    lane = lax.broadcasted_iota(jnp.int32, (half, LANE), 1)
    return jnp.where(lane < LANE - rest, here, there)


NAMES = ("phi", "first", "sums", "gain", "twiddle", "forward", "backward", "final", "coef")


def body_kernel(*refs):
    corr_ref, blend_ref, pad_ref, cutoff_ref, x_ref, flat_ref, dark_ref = refs[:7]
    tables = refs[7 : 7 + len(NAMES)]
    out_ref = refs[7 + len(NAMES)]
    rest = refs[8 + len(NAMES) :]
    held = rest[: len(NAMES)]
    (xs, got_s, gown_s, rs_s, sum_s, gx_s, bg_s, corr_s, edge_t, first_d,
     main_s, back_s, shift_s, yh_s, yl_s, res_s, edge_s,
     tsem, xsem, fsem, dsem, ex_send, ex_recv, rs_send, rs_recv, gx_send, gx_recv, ag_send, ag_recv,
     flat_s, dark_s) = rest[len(NAMES) :]
    phi_s, first_s, sums_s, gain_s, tw_s, fwd_s, bwd_s, fin_s, coef_s = held

    place = lax.axis_index("angle")
    row = lax.axis_index("row")
    halves = GROUP
    yy = lax.rem(place, halves)
    upper = place // halves
    half = LANE // 2
    wide = 2 * LANE
    blocks = flat_ref.shape[0]
    total = xs.shape[0] // blocks
    count = total // 2
    chunks = count // CHUNK
    length = 4 * blocks * LANE
    kept = length // 2
    reach = length * 3 // 4
    partner = (lax.rem(place + halves, 2 * halves), row)
    peers = [(upper * halves + lax.rem(yy + k, halves), row) for k in range(halves)]

    barrier = pltpu.get_barrier_semaphore()
    pl.semaphore_signal(barrier, inc=1, device_id=partner, device_id_type=MESH)
    for k in range(1, halves):
        pl.semaphore_signal(barrier, inc=1, device_id=peers[k], device_id_type=MESH)
    load_x = pltpu.make_async_copy(x_ref, xs, xsem)
    load_x.start()
    load_f = pltpu.make_async_copy(flat_ref, flat_s, fsem)
    load_f.start()
    load_d = pltpu.make_async_copy(dark_ref, dark_s, dsem)
    load_d.start()
    loads = [pltpu.make_async_copy(tables[i], held[i], tsem.at[i]) for i in range(len(NAMES))]
    for load in loads:
        load.start()
    pl.semaphore_wait(barrier, halves)

    span = CHUNK * blocks

    def exchange(c):
        return pltpu.make_async_remote_copy(
            src_ref=x_ref.at[pl.ds((1 - upper) * count * blocks + c * span, span), :],
            dst_ref=got_s.at[pl.ds(c * span, span), :],
            send_sem=ex_send.at[c],
            recv_sem=ex_recv.at[c],
            device_id=partner,
            device_id_type=MESH,
        )

    for c in range(chunks):
        exchange(c).start()

    block = GROUP * blocks

    def scatter(k):
        return pltpu.make_async_remote_copy(
            src_ref=gown_s.at[pl.ds(lax.rem(yy + k, halves) * block, block), :],
            dst_ref=rs_s.at[k],
            send_sem=rs_send.at[k],
            recv_sem=rs_recv.at[k],
            device_id=peers[k],
            device_id_type=MESH,
        )

    def across():
        return pltpu.make_async_remote_copy(
            src_ref=sum_s,
            dst_ref=gx_s,
            send_sem=gx_send,
            recv_sem=gx_recv,
            device_id=partner,
            device_id_type=MESH,
        )

    def gather(k):
        return pltpu.make_async_remote_copy(
            src_ref=bg_s.at[pl.ds(0, GROUP * half), :],
            dst_ref=bg_s.at[pl.ds(k * GROUP * half, GROUP * half), :],
            send_sem=ag_send.at[k],
            recv_sem=ag_recv.at[k],
            device_id=peers[k],
            device_id_type=MESH,
        )

    load_f.wait()
    load_d.wait()
    load_x.wait()
    for load in loads:
        load.wait()

    phi = phi_s[pl.ds(yy * MODES, MODES), :]
    for n1 in range(blocks):
        dark = dark_s[n1 : n1 + 1, :]
        base = jnp.log(flat_s[n1 : n1 + 1, :] - dark)
        rows = xs[pl.ds(n1, total, stride=blocks), :]
        high, low = split(base - jnp.log(rows - dark))
        gown_s[pl.ds(n1, MODES, stride=blocks), :] = dot(phi, jnp.concatenate([high, low, high], axis=0))
    for k in range(1, halves):
        scatter(k).start()

    corr = corr_ref[0]
    pad = pad_ref[0]
    blend = blend_ref[0].astype(jnp.float32)
    shift = blocks * LANE - corr
    q = lax.shift_right_logical(shift, 7)
    roll_by = jnp.bitwise_and(shift, LANE - 1)
    least = blocks - OVL_HI // LANE
    q = jnp.clip(q - least, 0, first_s.shape[0] // LANE - 1)
    first_d[...] = first_s[pl.ds(q * LANE, LANE), :]
    for which in range(2):
        tail = cut(sums_s, which, 1 - kept + corr + reach) - cut(sums_s, which, 1 - kept - pad + reach)
        ahead = cut(sums_s, which, 1 + pad + reach) - cut(sums_s, which, jnp.int32(1 + reach))
        edge_t[which * LANE : which * LANE + half, :] = tail
        edge_t[which * LANE + half : (which + 1) * LANE, :] = ahead
    shift_s[...] = jnp.zeros_like(shift_s)
    pixel = (
        lax.broadcasted_iota(jnp.int32, (blocks, LANE), 0) * LANE
        + lax.broadcasted_iota(jnp.int32, (blocks, LANE), 1)
    ).astype(jnp.float32)

    def step(v, carry):
        is_mode = v == MODE_STEP
        c = v - (v > MODE_STEP).astype(jnp.int32)

        @pl.when(v == MODE_STEP - 1)
        def _():
            for k in range(1, halves):
                scatter(k).wait()
            sum_s[...] = gown_s[pl.ds(yy * block, block), :] + rs_s[1] + rs_s[2] + rs_s[3]
            across().start()

        @pl.when(is_mode)
        def _():
            across().wait()
            mine = sum_s[...].reshape(GROUP, blocks, LANE)
            theirs = gx_s[...].reshape(GROUP, blocks, LANE)
            main_s[:GROUP] = jnp.where(upper == 1, theirs, mine)
            back_s[:GROUP] = jnp.where(upper == 1, mine, theirs)

        @pl.when(v == CORR_STEP)
        def _():
            for k in range(1, halves):
                gather(k).wait()
            coef = coef_s[pl.ds(place * count, count), :]
            for n1 in range(half):
                high, low = split(bg_s[pl.ds(n1, MODES, stride=half), :])
                corr_s[pl.ds(n1, count, stride=half), :] = dot(coef, jnp.concatenate([high, low, high], axis=0))

        @pl.when(jnp.logical_not(is_mode))
        def _():
            exchange(c).wait()
            dark = dark_s[...]
            base = jnp.log(flat_s[...] - dark)
            own = xs[pl.ds(upper * count * blocks + c * span, span), :].reshape(CHUNK, blocks, LANE)
            own = base - jnp.log(own - dark)
            got = base - jnp.log(got_s[pl.ds(c * span, span), :].reshape(CHUNK, blocks, LANE) - dark)
            main_s[...] = jnp.where(upper == 1, got, own)
            back_s[...] = jnp.where(upper == 1, own, got)

        weight = jnp.clip((pixel + 0.5 - corr.astype(jnp.float32) * 0.5) / blend + 0.5, 0.0, 1.0)
        lanes = lax.broadcasted_iota(jnp.int32, (blocks, LANE), 1)
        lanes48 = lax.broadcasted_iota(jnp.int32, (STACK - blocks, LANE), 1)
        for t in range(0, CHUNK, 2):
            parts = []
            for i in (t, t + 1):
                main = main_s[i]
                back = back_s[i]
                edge_s[0, i : i + 1, :] = jnp.broadcast_to(main[blocks - 1 : blocks, LANE - 1 :], (1, LANE))
                edge_s[1, i : i + 1, :] = jnp.broadcast_to(back[blocks - 1 : blocks, LANE - 1 :], (1, LANE))
                left = jnp.take_along_axis(back * weight, LANE - 1 - lanes, axis=1)
                shift_s[i, 8 : 8 + blocks, :] = pltpu.roll(main * weight, roll_by, 1)
                here = shift_s[i, 8 : 8 + STACK - blocks, :]
                prev = shift_s[i, 7 : 7 + STACK - blocks, :]
                right = jnp.where(lanes48 >= roll_by, here, prev)
                parts.append(jnp.concatenate([left, right], axis=0))
            high, low = split(jnp.concatenate(parts, axis=1))
            y = dot(first_d[...], jnp.concatenate([high, low, high], axis=0))
            cos, sin = tw_s[:half, :], tw_s[half:, :]
            for j, i in enumerate((t, t + 1)):
                re = y[:half, j * LANE : (j + 1) * LANE]
                im = y[half:, j * LANE : (j + 1) * LANE]
                turned = jnp.concatenate([re * cos + im * sin, im * cos - re * sin], axis=1)
                high, low = split(turned)
                yh_s[i * half : (i + 1) * half, :] = high
                yl_s[i * half : (i + 1) * half, :] = low
        which = is_mode.astype(jnp.int32)
        gain = gain_s[pl.ds(which * half, half), :]
        tail = edge_t[pl.ds(which * LANE, half), :]
        ahead = edge_t[pl.ds(which * LANE + half, half), :]
        gain2 = jnp.concatenate([gain, gain], axis=1)
        for t in range(0, CHUNK, 2):
            rows = slice(t * half, (t + 2) * half)
            z = (
                dot(yh_s[rows, :], fwd_s[:wide, :])
                + dot(yl_s[rows, :], fwd_s[:wide, :])
                + dot(yh_s[rows, :], fwd_s[wide:, :])
            )
            z = z * jnp.concatenate([gain2, gain2], axis=0)
            high, low = split(z)
            u = dot(high, bwd_s[:wide, :]) + dot(low, bwd_s[:wide, :]) + dot(high, bwd_s[wide:, :])
            parts = []
            cos, sin = tw_s[:half, :], tw_s[half:, :]
            for j in range(2):
                re = u[j * half : (j + 1) * half, :LANE]
                im = u[j * half : (j + 1) * half, LANE:]
                parts.append(jnp.concatenate([re * cos - im * sin, im * cos + re * sin], axis=0))
            high, low = split(jnp.concatenate(parts, axis=1))
            o = dot(fin_s[...], jnp.concatenate([high, low, high], axis=0))
            for j in range(2):
                i = t + j
                res_s[i] = (
                    o[:, j * LANE : (j + 1) * LANE]
                    + edge_s[0, i : i + 1, :] * tail
                    + edge_s[1, i : i + 1, :] * ahead
                )

        @pl.when(is_mode)
        def _():
            for i in range(GROUP):
                order = jnp.bitwise_and(yy * GROUP + i, KMAX - 1)
                keep = jnp.where(order < cutoff_ref[0], 1.0, 0.0)
                bg_s[i * half : (i + 1) * half, :] = res_s[i] * keep
            for k in range(1, halves):
                gather(k).start()

        @pl.when(jnp.logical_not(is_mode))
        def _():
            out_ref[pl.ds(c * CHUNK, CHUNK)] = res_s[...]

        return carry

    lax.fori_loop(0, chunks + 1, step, 0)

    def finish(i, carry):
        out_ref[i] = out_ref[i] + corr_s[pl.ds(i * half, half), :]
        return carry

    lax.fori_loop(0, count, finish, 0)


def local(intensity, flat_field, dark_field, correlation, blend_width, padding, cutoff):
    angle_count = lax.axis_size("angle")
    total = intensity.shape[0]
    count = total // 2
    pixels = intensity.shape[2]
    length = 4 * pixels
    blocks = pixels // LANE
    half = LANE // 2
    tables = constants(length, angle_count, total)
    tables = [jnp.asarray(tables[name]) for name in NAMES]
    block = GROUP * blocks
    peers = angle_count // 2
    f32, bf16 = jnp.float32, jnp.bfloat16
    dma = pltpu.SemaphoreType.DMA
    scratch = [pltpu.VMEM(t.shape, t.dtype) for t in tables] + [
        pltpu.VMEM((total * blocks, LANE), f32),
        pltpu.VMEM((count * blocks, LANE), f32),
        pltpu.VMEM((MODES * blocks, LANE), f32),
        pltpu.VMEM((peers, block, LANE), f32),
        pltpu.VMEM((block, LANE), f32),
        pltpu.VMEM((block, LANE), f32),
        pltpu.VMEM((MODES * half, LANE), f32),
        pltpu.VMEM((count * half, LANE), f32),
        pltpu.VMEM((4 * half, LANE), f32),
        pltpu.VMEM((LANE, 3 * STACK), bf16),
        pltpu.VMEM((CHUNK, blocks, LANE), f32),
        pltpu.VMEM((CHUNK, blocks, LANE), f32),
        pltpu.VMEM((CHUNK, STACK - blocks + 8, LANE), f32),
        pltpu.VMEM((CHUNK * half, 2 * LANE), bf16),
        pltpu.VMEM((CHUNK * half, 2 * LANE), bf16),
        pltpu.VMEM((CHUNK, half, LANE), f32),
        pltpu.VMEM((2, CHUNK, LANE), f32),
        dma((len(tables),)),
        dma,
        dma,
        dma,
        dma((count // CHUNK,)),
        dma((count // CHUNK,)),
        dma((peers,)),
        dma((peers,)),
        dma,
        dma,
        dma((peers,)),
        dma((peers,)),
        pltpu.VMEM((blocks, LANE), f32),
        pltpu.VMEM((blocks, LANE), f32),
    ]
    out = pl.pallas_call(
        body_kernel,
        out_shape=jax.ShapeDtypeStruct((count, half, LANE), f32),
        in_specs=[pl.BlockSpec(memory_space=pltpu.SMEM)] * 4
        + [pl.BlockSpec(memory_space=pl.ANY)] * (3 + len(tables)),
        out_specs=pl.BlockSpec(memory_space=pltpu.VMEM),
        scratch_shapes=scratch,
        compiler_params=pltpu.CompilerParams(
            vmem_limit_bytes=56 << 20, collective_id=0, has_side_effects=True
        ),
        name="filter_rows",
    )(
        correlation,
        blend_width,
        padding,
        cutoff,
        intensity.reshape(total * blocks, LANE),
        flat_field.reshape(blocks, LANE),
        dark_field.reshape(blocks, LANE),
        *tables,
    )
    return out.reshape(count, 1, 2 * pixels)


def solution(mesh):
    placed = (P("angle", "row", None), P("row", None), P("row", None), P(), P(), P(), P())
    return jax.shard_map(
        local, mesh=mesh, in_specs=placed, out_specs=P("angle", "row", None), check_vma=False
    )
```

```python
import functools

import jax
import jax.numpy as jnp
import numpy as np
from jax import lax
from jax.experimental import pallas as pl
from jax.experimental.pallas import tpu as pltpu
from jax.sharding import PartitionSpec as P

KMAX = 8
FCUT = 512
OVL_LO = 512
OVL_HI = 1536
LANE = 128
MODES = 16
GROUP = 4
CHUNK = 8
STACK = 80
SUM_STEP = 1
MODE_STEP = 3
CORR_STEP = 7
AHEAD = 2
MESH = pl.DeviceIdType.MESH


def split_np(table):
    high = table.astype(jnp.bfloat16)
    low = (table - high.astype(np.float64)).astype(jnp.bfloat16)
    return high, low


def split(value):
    high = value.astype(jnp.bfloat16)
    low = (value - high.astype(jnp.float32)).astype(jnp.bfloat16)
    return high, low


@functools.cache
def constants(length, angle_count, total):
    kept = length // 2
    freq = np.arange(kept, dtype=np.float64)
    ramp = freq / kept * (1.0 + np.cos(np.pi * freq / kept))
    drop = 1.0 - 1.0 / (1.0 + (freq / FCUT) ** 8)
    half = LANE // 2
    gains, sums = [], []
    reach = length * 3 // 4
    for gain in (ramp, ramp * drop):
        full = np.zeros(length)
        full[:kept] = gain
        full[kept + 1 :] = gain[:0:-1]
        kernel = np.fft.ifft(full).real
        offsets = np.arange(-reach, reach + 1)
        table = np.concatenate([[0.0], np.cumsum(kernel[offsets % length])])
        sums.append(np.pad(table, (0, -len(table) % LANE + LANE)).reshape(-1, LANE))
        place = np.arange(length)
        signed = np.where(place < kept, place, place - length)
        turned = kernel * np.exp(-1j * np.pi * signed / length)
        turned[kept] = 0.0
        between = np.fft.fft(turned).real
        k1 = np.arange(half)[:, None]
        k2 = np.arange(LANE)[None, :]
        gains.append(between[k1 + LANE * k2] * (2.0 / length))
    k1 = np.arange(half)[:, None]
    n2 = np.arange(LANE)[None, :]
    turn = 2.0 * np.pi * (k1 + 0.5) * n2 / length
    twiddle = np.stack([np.cos(turn), np.sin(turn)]).astype(np.float32)
    a = np.arange(LANE)[:, None]
    b = np.arange(LANE)[None, :]
    angle = 2.0 * np.pi * (a * b % LANE) / LANE
    c, s = np.cos(angle), np.sin(angle)
    forward = np.concatenate(split_np(np.block([[c, -s], [s, c]])), axis=0)
    backward = np.concatenate(split_np(np.block([[c, s], [-s, c]])), axis=0)
    n1 = np.arange(half)[:, None]
    last = 2.0 * np.pi * ((2 * np.arange(half)[None, :] + 1) * n1 % (2 * LANE)) / (2 * LANE)
    high, low = split_np(np.concatenate([np.cos(last), -np.sin(last)], axis=1))
    final = np.concatenate([high, high, low], axis=1)
    blocks = length // 4 // LANE
    firsts = []
    for q in range((length // 4 - OVL_HI) // LANE, (length // 4 - OVL_LO) // LANE + 1):
        index = np.concatenate([blocks - 1 - np.arange(blocks), q + np.arange(STACK - blocks)])[None, :]
        turn = np.pi * ((2 * k1 + 1) * index % (2 * LANE)) / LANE
        high, low = split_np(np.concatenate([np.cos(turn), -np.sin(turn)], axis=0))
        firsts.append(np.concatenate([high, high, low], axis=1))
    halves = angle_count // 2
    half_turn = angle_count * total // 2
    orders = np.arange(KMAX)[:, None]
    phis, coefs = [], []
    for place in range(angle_count):
        base = place % halves * total
        turn = 2.0 * np.pi * (orders * (base + np.arange(total)[None, :]) % half_turn) / half_turn
        table = np.concatenate([np.cos(turn), np.sin(turn)], axis=0)
        if place < halves:
            high, low = split_np(table)
            phis.append(np.concatenate([high, high, low], axis=1))
        start = place // halves * (total // 2)
        table = table[:, start : start + total // 2] * (-2.0 / half_turn)
        table[0] *= 0.5
        groups = table.reshape(halves, GROUP, -1)
        table = np.concatenate([groups[(place % halves - k) % halves] for k in range(halves)], axis=0)
        high, low = split_np(table.T)
        coefs.append(np.concatenate([high, high, low], axis=1))
    return dict(
        phi=np.concatenate(phis, axis=0),
        first=np.concatenate(firsts, axis=0),
        sums=np.concatenate(sums, axis=0).astype(np.float32),
        gain=np.concatenate(gains, axis=0).astype(np.float32),
        twiddle=twiddle.reshape(2 * half, LANE),
        forward=forward,
        backward=backward,
        final=final,
        coef=np.concatenate(coefs, axis=0),
    )


def dot(a, b):
    return jnp.dot(a, b, preferred_element_type=jnp.float32)


def cut(sums_s, which, start):
    half = LANE // 2
    rows = sums_s.shape[0] // 2
    row = lax.shift_right_logical(start, 7)
    rest = jnp.bitwise_and(start, LANE - 1)
    back = jnp.bitwise_and(LANE - rest, LANE - 1)
    here = pltpu.roll(sums_s[pl.ds(which * rows + row, half), :], back, 1)
    there = pltpu.roll(sums_s[pl.ds(which * rows + row + 1, half), :], back, 1)
    lane = lax.broadcasted_iota(jnp.int32, (half, LANE), 1)
    return jnp.where(lane < LANE - rest, here, there)


NAMES = ("phi", "first", "sums", "gain", "twiddle", "forward", "backward", "final", "coef")


def body_kernel(*refs):
    corr_ref, blend_ref, pad_ref, cutoff_ref, x_ref, flat_ref, dark_ref = refs[:7]
    tables = refs[7 : 7 + len(NAMES)]
    out_ref = refs[7 + len(NAMES)]
    rest = refs[8 + len(NAMES) :]
    held = rest[: len(NAMES)]
    (xs, got_s, gown_s, rs_s, sum_s, gx_s, bg_s, corr_s, edge_t, first_d,
     main_s, back_s, shift_s, yh_s, yl_s, res_s, edge_s,
     tsem, xsem, fsem, dsem, ex_send, ex_recv, rs_send, rs_recv, gx_send, gx_recv, ag_send, ag_recv,
     flat_s, dark_s) = rest[len(NAMES) :]
    phi_s, first_s, sums_s, gain_s, tw_s, fwd_s, bwd_s, fin_s, coef_s = held

    place = lax.axis_index("angle")
    row = lax.axis_index("row")
    halves = GROUP
    yy = lax.rem(place, halves)
    upper = place // halves
    half = LANE // 2
    wide = 2 * LANE
    blocks = flat_ref.shape[0]
    total = xs.shape[0] // blocks
    count = total // 2
    chunks = count // CHUNK
    length = 4 * blocks * LANE
    kept = length // 2
    reach = length * 3 // 4
    partner = (lax.rem(place + halves, 2 * halves), row)
    peers = [(upper * halves + lax.rem(yy + k, halves), row) for k in range(halves)]

    barrier = pltpu.get_barrier_semaphore()
    pl.semaphore_signal(barrier, inc=1, device_id=partner, device_id_type=MESH)
    for k in range(1, halves):
        pl.semaphore_signal(barrier, inc=1, device_id=peers[k], device_id_type=MESH)
    load_x = pltpu.make_async_copy(x_ref, xs, xsem)
    load_x.start()
    load_f = pltpu.make_async_copy(flat_ref, flat_s, fsem)
    load_f.start()
    load_d = pltpu.make_async_copy(dark_ref, dark_s, dsem)
    load_d.start()
    loads = [pltpu.make_async_copy(tables[i], held[i], tsem.at[i]) for i in range(len(NAMES))]
    for load in loads:
        load.start()
    pl.semaphore_wait(barrier, halves)

    span = CHUNK * blocks

    def exchange(c):
        return pltpu.make_async_remote_copy(
            src_ref=x_ref.at[pl.ds((1 - upper) * count * blocks + c * span, span), :],
            dst_ref=got_s.at[pl.ds(c * span, span), :],
            send_sem=ex_send.at[c],
            recv_sem=ex_recv.at[c],
            device_id=partner,
            device_id_type=MESH,
        )

    for c in range(AHEAD):
        exchange(c).start()

    block = GROUP * blocks

    def scatter(k):
        return pltpu.make_async_remote_copy(
            src_ref=gown_s.at[pl.ds(lax.rem(yy + k, halves) * block, block), :],
            dst_ref=rs_s.at[k],
            send_sem=rs_send.at[k],
            recv_sem=rs_recv.at[k],
            device_id=peers[k],
            device_id_type=MESH,
        )

    def across():
        return pltpu.make_async_remote_copy(
            src_ref=sum_s,
            dst_ref=gx_s,
            send_sem=gx_send,
            recv_sem=gx_recv,
            device_id=partner,
            device_id_type=MESH,
        )

    def gather(k):
        return pltpu.make_async_remote_copy(
            src_ref=bg_s.at[pl.ds(0, GROUP * half), :],
            dst_ref=bg_s.at[pl.ds(k * GROUP * half, GROUP * half), :],
            send_sem=ag_send.at[k],
            recv_sem=ag_recv.at[k],
            device_id=peers[k],
            device_id_type=MESH,
        )

    load_f.wait()
    load_d.wait()
    load_x.wait()
    for load in loads:
        load.wait()

    phi = phi_s[pl.ds(yy * MODES, MODES), :]
    for n1 in range(blocks):
        dark = dark_s[n1 : n1 + 1, :]
        base = jnp.log(flat_s[n1 : n1 + 1, :] - dark)
        rows = xs[pl.ds(n1, total, stride=blocks), :]
        high, low = split(base - jnp.log(rows - dark))
        gown_s[pl.ds(n1, MODES, stride=blocks), :] = dot(phi, jnp.concatenate([high, low, high], axis=0))
    for k in range(1, halves):
        scatter(k).start()

    corr = corr_ref[0]
    pad = pad_ref[0]
    blend = blend_ref[0].astype(jnp.float32)
    shift = blocks * LANE - corr
    q = lax.shift_right_logical(shift, 7)
    roll_by = jnp.bitwise_and(shift, LANE - 1)
    least = blocks - OVL_HI // LANE
    q = jnp.clip(q - least, 0, first_s.shape[0] // LANE - 1)
    first_d[...] = first_s[pl.ds(q * LANE, LANE), :]
    for which in range(2):
        tail = cut(sums_s, which, 1 - kept + corr + reach) - cut(sums_s, which, 1 - kept - pad + reach)
        ahead = cut(sums_s, which, 1 + pad + reach) - cut(sums_s, which, jnp.int32(1 + reach))
        edge_t[which * LANE : which * LANE + half, :] = tail
        edge_t[which * LANE + half : (which + 1) * LANE, :] = ahead
    shift_s[...] = jnp.zeros_like(shift_s)
    pixel = (
        lax.broadcasted_iota(jnp.int32, (blocks, LANE), 0) * LANE
        + lax.broadcasted_iota(jnp.int32, (blocks, LANE), 1)
    ).astype(jnp.float32)

    def step(v, carry):
        is_mode = v == MODE_STEP
        c = v - (v > MODE_STEP).astype(jnp.int32)

        @pl.when(v == SUM_STEP)
        def _():
            for k in range(1, halves):
                scatter(k).wait()
            sum_s[...] = gown_s[pl.ds(yy * block, block), :] + rs_s[1] + rs_s[2] + rs_s[3]
            across().start()

        @pl.when(is_mode)
        def _():
            across().wait()
            mine = sum_s[...].reshape(GROUP, blocks, LANE)
            theirs = gx_s[...].reshape(GROUP, blocks, LANE)
            main_s[:GROUP] = jnp.where(upper == 1, theirs, mine)
            back_s[:GROUP] = jnp.where(upper == 1, mine, theirs)

        @pl.when(v == CORR_STEP)
        def _():
            for k in range(1, halves):
                gather(k).wait()
            coef = coef_s[pl.ds(place * count, count), :]
            for n1 in range(half):
                high, low = split(bg_s[pl.ds(n1, MODES, stride=half), :])
                corr_s[pl.ds(n1, count, stride=half), :] = dot(coef, jnp.concatenate([high, low, high], axis=0))

            def mend(i, carry):
                out_ref[i] = out_ref[i] + corr_s[pl.ds(i * half, half), :]
                return carry

            lax.fori_loop(0, (CORR_STEP - 1) * CHUNK, mend, 0)

        @pl.when(jnp.logical_not(is_mode))
        def _():
            exchange(c).wait()

            @pl.when(c + AHEAD < chunks)
            def _():
                exchange(c + AHEAD).start()

            dark = dark_s[...]
            base = jnp.log(flat_s[...] - dark)
            own = xs[pl.ds(upper * count * blocks + c * span, span), :].reshape(CHUNK, blocks, LANE)
            own = base - jnp.log(own - dark)
            got = base - jnp.log(got_s[pl.ds(c * span, span), :].reshape(CHUNK, blocks, LANE) - dark)
            main_s[...] = jnp.where(upper == 1, got, own)
            back_s[...] = jnp.where(upper == 1, own, got)

        weight = jnp.clip((pixel + 0.5 - corr.astype(jnp.float32) * 0.5) / blend + 0.5, 0.0, 1.0)
        lanes = lax.broadcasted_iota(jnp.int32, (blocks, LANE), 1)
        lanes48 = lax.broadcasted_iota(jnp.int32, (STACK - blocks, LANE), 1)
        for t in range(0, CHUNK, 2):
            parts = []
            for i in (t, t + 1):
                main = main_s[i]
                back = back_s[i]
                edge_s[0, i : i + 1, :] = jnp.broadcast_to(main[blocks - 1 : blocks, LANE - 1 :], (1, LANE))
                edge_s[1, i : i + 1, :] = jnp.broadcast_to(back[blocks - 1 : blocks, LANE - 1 :], (1, LANE))
                left = jnp.take_along_axis(back * weight, LANE - 1 - lanes, axis=1)
                shift_s[i, 8 : 8 + blocks, :] = pltpu.roll(main * weight, roll_by, 1)
                here = shift_s[i, 8 : 8 + STACK - blocks, :]
                prev = shift_s[i, 7 : 7 + STACK - blocks, :]
                right = jnp.where(lanes48 >= roll_by, here, prev)
                parts.append(jnp.concatenate([left, right], axis=0))
            high, low = split(jnp.concatenate(parts, axis=1))
            y = dot(first_d[...], jnp.concatenate([high, low, high], axis=0))
            cos, sin = tw_s[:half, :], tw_s[half:, :]
            for j, i in enumerate((t, t + 1)):
                re = y[:half, j * LANE : (j + 1) * LANE]
                im = y[half:, j * LANE : (j + 1) * LANE]
                turned = jnp.concatenate([re * cos + im * sin, im * cos - re * sin], axis=1)
                high, low = split(turned)
                yh_s[i * half : (i + 1) * half, :] = high
                yl_s[i * half : (i + 1) * half, :] = low
        which = is_mode.astype(jnp.int32)
        gain = gain_s[pl.ds(which * half, half), :]
        tail = edge_t[pl.ds(which * LANE, half), :]
        ahead = edge_t[pl.ds(which * LANE + half, half), :]
        gain2 = jnp.concatenate([gain, gain], axis=1)
        for t in range(0, CHUNK, 2):
            rows = slice(t * half, (t + 2) * half)
            z = (
                dot(yh_s[rows, :], fwd_s[:wide, :])
                + dot(yl_s[rows, :], fwd_s[:wide, :])
                + dot(yh_s[rows, :], fwd_s[wide:, :])
            )
            z = z * jnp.concatenate([gain2, gain2], axis=0)
            high, low = split(z)
            u = dot(high, bwd_s[:wide, :]) + dot(low, bwd_s[:wide, :]) + dot(high, bwd_s[wide:, :])
            parts = []
            cos, sin = tw_s[:half, :], tw_s[half:, :]
            for j in range(2):
                re = u[j * half : (j + 1) * half, :LANE]
                im = u[j * half : (j + 1) * half, LANE:]
                parts.append(jnp.concatenate([re * cos - im * sin, im * cos + re * sin], axis=0))
            high, low = split(jnp.concatenate(parts, axis=1))
            o = dot(fin_s[...], jnp.concatenate([high, low, high], axis=0))
            for j in range(2):
                i = t + j
                res_s[i] = (
                    o[:, j * LANE : (j + 1) * LANE]
                    + edge_s[0, i : i + 1, :] * tail
                    + edge_s[1, i : i + 1, :] * ahead
                )

        @pl.when(is_mode)
        def _():
            for i in range(GROUP):
                order = jnp.bitwise_and(yy * GROUP + i, KMAX - 1)
                keep = jnp.where(order < cutoff_ref[0], 1.0, 0.0)
                bg_s[i * half : (i + 1) * half, :] = res_s[i] * keep
            for k in range(1, halves):
                gather(k).start()

        @pl.when(jnp.logical_and(jnp.logical_not(is_mode), v < CORR_STEP))
        def _():
            out_ref[pl.ds(c * CHUNK, CHUNK)] = res_s[...]

        @pl.when(v >= CORR_STEP)
        def _():
            rows = corr_s[pl.ds(c * CHUNK * half, CHUNK * half), :]
            out_ref[pl.ds(c * CHUNK, CHUNK)] = res_s[...] + rows.reshape(CHUNK, half, LANE)

        return carry

    lax.fori_loop(0, chunks + 1, step, 0)


def local(intensity, flat_field, dark_field, correlation, blend_width, padding, cutoff):
    angle_count = lax.axis_size("angle")
    total = intensity.shape[0]
    count = total // 2
    pixels = intensity.shape[2]
    length = 4 * pixels
    blocks = pixels // LANE
    half = LANE // 2
    tables = constants(length, angle_count, total)
    tables = [jnp.asarray(tables[name]) for name in NAMES]
    block = GROUP * blocks
    peers = angle_count // 2
    f32, bf16 = jnp.float32, jnp.bfloat16
    dma = pltpu.SemaphoreType.DMA
    scratch = [pltpu.VMEM(t.shape, t.dtype) for t in tables] + [
        pltpu.VMEM((total * blocks, LANE), f32),
        pltpu.VMEM((count * blocks, LANE), f32),
        pltpu.VMEM((MODES * blocks, LANE), f32),
        pltpu.VMEM((peers, block, LANE), f32),
        pltpu.VMEM((block, LANE), f32),
        pltpu.VMEM((block, LANE), f32),
        pltpu.VMEM((MODES * half, LANE), f32),
        pltpu.VMEM((count * half, LANE), f32),
        pltpu.VMEM((4 * half, LANE), f32),
        pltpu.VMEM((LANE, 3 * STACK), bf16),
        pltpu.VMEM((CHUNK, blocks, LANE), f32),
        pltpu.VMEM((CHUNK, blocks, LANE), f32),
        pltpu.VMEM((CHUNK, STACK - blocks + 8, LANE), f32),
        pltpu.VMEM((CHUNK * half, 2 * LANE), bf16),
        pltpu.VMEM((CHUNK * half, 2 * LANE), bf16),
        pltpu.VMEM((CHUNK, half, LANE), f32),
        pltpu.VMEM((2, CHUNK, LANE), f32),
        dma((len(tables),)),
        dma,
        dma,
        dma,
        dma((count // CHUNK,)),
        dma((count // CHUNK,)),
        dma((peers,)),
        dma((peers,)),
        dma,
        dma,
        dma((peers,)),
        dma((peers,)),
        pltpu.VMEM((blocks, LANE), f32),
        pltpu.VMEM((blocks, LANE), f32),
    ]
    out = pl.pallas_call(
        body_kernel,
        out_shape=jax.ShapeDtypeStruct((count, half, LANE), f32),
        in_specs=[pl.BlockSpec(memory_space=pltpu.SMEM)] * 4
        + [pl.BlockSpec(memory_space=pltpu.HBM)] * (3 + len(tables)),
        out_specs=pl.BlockSpec(memory_space=pltpu.VMEM),
        scratch_shapes=scratch,
        compiler_params=pltpu.CompilerParams(
            vmem_limit_bytes=20 << 20, collective_id=0, has_side_effects=True
        ),
        name="filter_rows",
    )(
        correlation,
        blend_width,
        padding,
        cutoff,
        *[
            pltpu.with_memory_space_constraint(a, pltpu.HBM)
            for a in (
                intensity.reshape(total * blocks, LANE),
                flat_field.reshape(blocks, LANE),
                dark_field.reshape(blocks, LANE),
                *tables,
            )
        ],
    )
    return out.reshape(count, 1, 2 * pixels)


def solution(mesh):
    placed = (P("angle", "row", None), P("row", None), P("row", None), P(), P(), P(), P())
    return jax.shard_map(
        local, mesh=mesh, in_specs=placed, out_specs=P("angle", "row", None), check_vma=False
    )
```

```python
import functools

import jax
import jax.numpy as jnp
import numpy as np
from jax import lax
from jax.experimental import pallas as pl
from jax.experimental.pallas import tpu as pltpu
from jax.sharding import PartitionSpec as P

KMAX = 8
FCUT = 512
OVL_LO = 512
OVL_HI = 1536
LANE = 128
MODES = 16
GROUP = 4
CHUNK = 8
STACK = 80
SUM_STEP = 1
MODE_STEP = 3
CORR_STEP = 6
FIRST = 3
AHEAD = 4
MESH = pl.DeviceIdType.MESH


def split_np(table):
    high = table.astype(jnp.bfloat16)
    low = (table - high.astype(np.float64)).astype(jnp.bfloat16)
    return high, low


def split(value):
    high = value.astype(jnp.bfloat16)
    low = (value - high.astype(jnp.float32)).astype(jnp.bfloat16)
    return high, low


@functools.cache
def constants(length, angle_count, total):
    kept = length // 2
    freq = np.arange(kept, dtype=np.float64)
    ramp = freq / kept * (1.0 + np.cos(np.pi * freq / kept))
    drop = 1.0 - 1.0 / (1.0 + (freq / FCUT) ** 8)
    half = LANE // 2
    gains, sums = [], []
    reach = length * 3 // 4
    for gain in (ramp, ramp * drop):
        full = np.zeros(length)
        full[:kept] = gain
        full[kept + 1 :] = gain[:0:-1]
        kernel = np.fft.ifft(full).real
        offsets = np.arange(-reach, reach + 1)
        table = np.concatenate([[0.0], np.cumsum(kernel[offsets % length])])
        sums.append(np.pad(table, (0, -len(table) % LANE + LANE)).reshape(-1, LANE))
        place = np.arange(length)
        signed = np.where(place < kept, place, place - length)
        turned = kernel * np.exp(-1j * np.pi * signed / length)
        turned[kept] = 0.0
        between = np.fft.fft(turned).real
        k1 = np.arange(half)[:, None]
        k2 = np.arange(LANE)[None, :]
        gains.append(between[k1 + LANE * k2] * (2.0 / length))
    k1 = np.arange(half)[:, None]
    n2 = np.arange(LANE)[None, :]
    turn = 2.0 * np.pi * (k1 + 0.5) * n2 / length
    twiddle = np.stack([np.cos(turn), np.sin(turn)]).astype(np.float32)
    a = np.arange(LANE)[:, None]
    b = np.arange(LANE)[None, :]
    angle = 2.0 * np.pi * (a * b % LANE) / LANE
    c, s = np.cos(angle), np.sin(angle)
    high, low = split_np(np.block([[c, -s], [s, c]]))
    forward = np.concatenate([high, high, low], axis=0)
    high, low = split_np(np.block([[c, s], [-s, c]]))
    backward = np.concatenate([high, high, low], axis=0)
    n1 = np.arange(half)[:, None]
    last = 2.0 * np.pi * ((2 * np.arange(half)[None, :] + 1) * n1 % (2 * LANE)) / (2 * LANE)
    high, low = split_np(np.concatenate([np.cos(last), -np.sin(last)], axis=1))
    final = np.concatenate([high, high, low], axis=1)
    blocks = length // 4 // LANE
    firsts = []
    for q in range((length // 4 - OVL_HI) // LANE, (length // 4 - OVL_LO) // LANE + 1):
        index = np.concatenate([blocks - 1 - np.arange(blocks), q + np.arange(STACK - blocks)])[None, :]
        turn = np.pi * ((2 * k1 + 1) * index % (2 * LANE)) / LANE
        high, low = split_np(np.concatenate([np.cos(turn), -np.sin(turn)], axis=0))
        firsts.append(np.concatenate([high, high, low], axis=1))
    halves = angle_count // 2
    half_turn = angle_count * total // 2
    orders = np.arange(KMAX)[:, None]
    phis, coefs = [], []
    for place in range(angle_count):
        base = place % halves * total
        turn = 2.0 * np.pi * (orders * (base + np.arange(total)[None, :]) % half_turn) / half_turn
        table = np.concatenate([np.cos(turn), np.sin(turn)], axis=0)
        if place < halves:
            high, low = split_np(table)
            phis.append(np.concatenate([high, high, low], axis=1))
        start = place // halves * (total // 2)
        table = table[:, start : start + total // 2] * (-2.0 / half_turn)
        table[0] *= 0.5
        groups = table.reshape(halves, GROUP, -1)
        table = np.concatenate([groups[(place % halves - k) % halves] for k in range(halves)], axis=0)
        high, low = split_np(table.T)
        coefs.append(np.concatenate([high, high, low], axis=1))
    return dict(
        phi=np.concatenate(phis, axis=0),
        first=np.concatenate(firsts, axis=0),
        sums=np.concatenate(sums, axis=0).astype(np.float32),
        gain=np.concatenate(gains, axis=0).astype(np.float32),
        twiddle=twiddle.reshape(2 * half, LANE),
        forward=forward,
        backward=backward,
        final=final,
        coef=np.concatenate(coefs, axis=0),
    )


def dot(a, b):
    return jnp.dot(a, b, preferred_element_type=jnp.float32)


def cut(sums_s, which, start):
    half = LANE // 2
    rows = sums_s.shape[0] // 2
    row = lax.shift_right_logical(start, 7)
    rest = jnp.bitwise_and(start, LANE - 1)
    back = jnp.bitwise_and(LANE - rest, LANE - 1)
    here = pltpu.roll(sums_s[pl.ds(which * rows + row, half), :], back, 1)
    there = pltpu.roll(sums_s[pl.ds(which * rows + row + 1, half), :], back, 1)
    lane = lax.broadcasted_iota(jnp.int32, (half, LANE), 1)
    return jnp.where(lane < LANE - rest, here, there)


SCRATCH_NAMES = ("phi", "first", "sums", "gain", "forward", "coef")
NAMES = SCRATCH_NAMES + ("twiddle", "backward", "final")


def inverse(zk_s, bwd_s, fin_s, tw_s, uk_s):
    half = LANE // 2
    u = dot(zk_s[...], bwd_s[...])
    cos, sin = tw_s[:half, :], tw_s[half:, :]
    for i in range(CHUNK):
        re = u[i * half : (i + 1) * half, :LANE]
        im = u[i * half : (i + 1) * half, LANE:]
        high, low = split(jnp.concatenate([re * cos - im * sin, im * cos + re * sin], axis=0))
        cols = slice(i * LANE, (i + 1) * LANE)
        uk_s[:LANE, cols] = high
        uk_s[LANE : 2 * LANE, cols] = low
        uk_s[2 * LANE :, cols] = high
    return dot(fin_s[...], uk_s[...])


def finish_kernel(out_ref, zk_ref, bias_ref, bwd_ref, fin_ref, tw_ref, y_ref, uk_s, res_s, sems):
    done = out_ref.shape[0]
    part = done // (sems.shape[0] - 1)
    copies = [
        pltpu.make_async_copy(
            out_ref.at[pl.ds(i * part, part)], y_ref.at[pl.ds(i * part, part)], sems.at[i]
        )
        for i in range(done // part)
    ]
    for copy in copies:
        copy.start()
    o = inverse(zk_ref, bwd_ref, fin_ref, tw_ref, uk_s)
    for i in range(CHUNK):
        res_s[i] = o[:, i * LANE : (i + 1) * LANE] + bias_ref[i]
    last = pltpu.make_async_copy(res_s, y_ref.at[pl.ds(done, CHUNK)], sems.at[done // part])
    last.start()
    for copy in copies:
        copy.wait()
    last.wait()


def body_kernel(*refs):
    scalar_refs, (x_ref, flat_ref, dark_ref) = refs[:4], refs[4:7]
    tables = refs[7 : 7 + len(NAMES)]
    out_ref, zk_o, bias_o, bwd_s, fin_s, tw_s = refs[7 + len(NAMES) : 13 + len(NAMES)]
    rest = refs[13 + len(NAMES) :]
    (xs, got_s, gown_s, rs_s, sum_s, gx_s, bg_s, corr_s, edge_t, first_d,
     main_s, back_s, shift_s, xk_s, yk_s, zk_s, uk_s, res_s, edge_s,
     tsem, xsem, fsem, dsem, ex_send, ex_recv, rs_send, rs_recv, gx_send, gx_recv, ag_send, ag_recv,
     flat_s, dark_s) = rest[len(SCRATCH_NAMES) :]
    phi_s, first_s, sums_s, gain_s, fwd_s, coef_s = rest[: len(SCRATCH_NAMES)]
    held = (phi_s, first_s, sums_s, gain_s, fwd_s, coef_s, tw_s, bwd_s, fin_s)

    place = lax.axis_index("angle")
    row = lax.axis_index("row")
    halves = GROUP
    yy = lax.rem(place, halves)
    upper = place // halves
    half = LANE // 2
    wide = 2 * LANE
    blocks = flat_ref.shape[0]
    total = xs.shape[0] // blocks
    count = total // 2
    chunks = count // CHUNK
    length = 4 * blocks * LANE
    kept = length // 2
    reach = length * 3 // 4
    partner = (lax.rem(place + halves, 2 * halves), row)
    peers = [(upper * halves + lax.rem(yy + k, halves), row) for k in range(halves)]

    barrier = pltpu.get_barrier_semaphore()
    pl.semaphore_signal(barrier, inc=1, device_id=partner, device_id_type=MESH)
    for k in range(1, halves):
        pl.semaphore_signal(barrier, inc=1, device_id=peers[k], device_id_type=MESH)
    load_x = pltpu.make_async_copy(x_ref, xs, xsem)
    load_x.start()
    load_f = pltpu.make_async_copy(flat_ref, flat_s, fsem)
    load_f.start()
    load_d = pltpu.make_async_copy(dark_ref, dark_s, dsem)
    load_d.start()
    loads = [pltpu.make_async_copy(tables[i], held[i], tsem.at[i]) for i in range(len(NAMES))]
    corr_ref, blend_ref, pad_ref, cutoff_ref = scalar_refs
    pl.semaphore_wait(barrier, halves)

    span = CHUNK * blocks

    def exchange(c):
        return pltpu.make_async_remote_copy(
            src_ref=x_ref.at[pl.ds((1 - upper) * count * blocks + c * span, span), :],
            dst_ref=got_s.at[pl.ds(c * span, span), :],
            send_sem=ex_send.at[c],
            recv_sem=ex_recv.at[c],
            device_id=partner,
            device_id_type=MESH,
        )

    for c in range(FIRST):
        exchange(c).start()
    for load in loads:
        load.start()

    block = GROUP * blocks

    def scatter(k):
        return pltpu.make_async_remote_copy(
            src_ref=gown_s.at[pl.ds(lax.rem(yy + k, halves) * block, block), :],
            dst_ref=rs_s.at[k],
            send_sem=rs_send.at[k],
            recv_sem=rs_recv.at[k],
            device_id=peers[k],
            device_id_type=MESH,
        )

    def across():
        return pltpu.make_async_remote_copy(
            src_ref=sum_s,
            dst_ref=gx_s,
            send_sem=gx_send,
            recv_sem=gx_recv,
            device_id=partner,
            device_id_type=MESH,
        )

    def gather(k):
        return pltpu.make_async_remote_copy(
            src_ref=bg_s.at[pl.ds(0, GROUP * half), :],
            dst_ref=bg_s.at[pl.ds(k * GROUP * half, GROUP * half), :],
            send_sem=ag_send.at[k],
            recv_sem=ag_recv.at[k],
            device_id=peers[k],
            device_id_type=MESH,
        )

    load_f.wait()
    load_d.wait()
    load_x.wait()
    for load in loads:
        load.wait()

    phi = phi_s[pl.ds(yy * MODES, MODES), :]
    for n1 in range(blocks):
        dark = dark_s[n1 : n1 + 1, :]
        base = jnp.log(flat_s[n1 : n1 + 1, :] - dark)
        rows = xs[pl.ds(n1, total, stride=blocks), :]
        high, low = split(base - jnp.log(rows - dark))
        gown_s[pl.ds(n1, MODES, stride=blocks), :] = dot(phi, jnp.concatenate([high, low, high], axis=0))
    for k in range(1, halves):
        scatter(k).start()

    corr = corr_ref[0]
    pad = pad_ref[0]
    blend = blend_ref[0].astype(jnp.float32)
    shift = blocks * LANE - corr
    q = lax.shift_right_logical(shift, 7)
    roll_by = jnp.bitwise_and(shift, LANE - 1)
    least = blocks - OVL_HI // LANE
    q = jnp.clip(q - least, 0, first_s.shape[0] // LANE - 1)
    first_d[...] = first_s[pl.ds(q * LANE, LANE), :]
    for which in range(2):
        tail = cut(sums_s, which, 1 - kept + corr + reach) - cut(sums_s, which, 1 - kept - pad + reach)
        ahead = cut(sums_s, which, 1 + pad + reach) - cut(sums_s, which, jnp.int32(1 + reach))
        edge_t[which * LANE : which * LANE + half, :] = tail
        edge_t[which * LANE + half : (which + 1) * LANE, :] = ahead
    shift_s[...] = jnp.zeros_like(shift_s)
    pixel = (
        lax.broadcasted_iota(jnp.int32, (blocks, LANE), 0) * LANE
        + lax.broadcasted_iota(jnp.int32, (blocks, LANE), 1)
    ).astype(jnp.float32)

    def receive(c):
        exchange(c).wait()

        @pl.when(False if isinstance(c, int) else jnp.logical_and(c >= SUM_STEP, c + AHEAD < chunks))
        def _():
            exchange(c + AHEAD).start()

        dark = dark_s[...]
        base = jnp.log(flat_s[...] - dark)
        own = xs[pl.ds(upper * count * blocks + c * span, span), :].reshape(CHUNK, blocks, LANE)
        own = base - jnp.log(own - dark)
        got = base - jnp.log(got_s[pl.ds(c * span, span), :].reshape(CHUNK, blocks, LANE) - dark)
        main_s[...] = jnp.where(upper == 1, got, own)
        back_s[...] = jnp.where(upper == 1, own, got)

    def front(which, zk_s):
        weight = jnp.clip((pixel + 0.5 - corr.astype(jnp.float32) * 0.5) / blend + 0.5, 0.0, 1.0)
        lanes = lax.broadcasted_iota(jnp.int32, (blocks, LANE), 1)
        lanes48 = lax.broadcasted_iota(jnp.int32, (STACK - blocks, LANE), 1)
        for i in range(CHUNK):
            main = main_s[i]
            back = back_s[i]
            edge_s[0, i : i + 1, :] = jnp.broadcast_to(main[blocks - 1 : blocks, LANE - 1 :], (1, LANE))
            edge_s[1, i : i + 1, :] = jnp.broadcast_to(back[blocks - 1 : blocks, LANE - 1 :], (1, LANE))
            left = jnp.take_along_axis(back * weight, LANE - 1 - lanes, axis=1)
            shift_s[i, 8 : 8 + blocks, :] = pltpu.roll(main * weight, roll_by, 1)
            here = shift_s[i, 8 : 8 + STACK - blocks, :]
            prev = shift_s[i, 7 : 7 + STACK - blocks, :]
            right = jnp.where(lanes48 >= roll_by, here, prev)
            high, low = split(jnp.concatenate([left, right], axis=0))
            cols = slice(i * LANE, (i + 1) * LANE)
            xk_s[:STACK, cols] = high
            xk_s[STACK : 2 * STACK, cols] = low
            xk_s[2 * STACK :, cols] = high
        y = dot(first_d[...], xk_s[...])
        cos, sin = tw_s[:half, :], tw_s[half:, :]
        for i in range(CHUNK):
            re = y[:half, i * LANE : (i + 1) * LANE]
            im = y[half:, i * LANE : (i + 1) * LANE]
            high, low = split(jnp.concatenate([re * cos + im * sin, im * cos - re * sin], axis=1))
            rows = slice(i * half, (i + 1) * half)
            yk_s[rows, :wide] = high
            yk_s[rows, wide : 2 * wide] = low
            yk_s[rows, 2 * wide :] = high
        gain = gain_s[pl.ds(which * half, half), :]
        gain2 = jnp.concatenate([gain, gain], axis=1)
        z = dot(yk_s[...], fwd_s[...])
        for i in range(CHUNK):
            rows = slice(i * half, (i + 1) * half)
            high, low = split(z[rows] * gain2)
            zk_s[rows, :wide] = high
            zk_s[rows, wide : 2 * wide] = low
            zk_s[rows, 2 * wide :] = high

    def edges(which, i):
        tail = edge_t[pl.ds(which * LANE, half), :]
        ahead = edge_t[pl.ds(which * LANE + half, half), :]
        return edge_s[0, i : i + 1, :] * tail + edge_s[1, i : i + 1, :] * ahead

    def step(v, carry):
        is_mode = v == MODE_STEP
        c = v - (v > MODE_STEP).astype(jnp.int32)

        @pl.when(v == SUM_STEP)
        def _():
            for k in range(1, halves):
                scatter(k).wait()
            sum_s[...] = gown_s[pl.ds(yy * block, block), :] + rs_s[1] + rs_s[2] + rs_s[3]
            across().start()
            for c in range(FIRST, AHEAD + SUM_STEP):
                exchange(c).start()

        @pl.when(is_mode)
        def _():
            across().wait()
            mine = sum_s[...].reshape(GROUP, blocks, LANE)
            theirs = gx_s[...].reshape(GROUP, blocks, LANE)
            main_s[:GROUP] = jnp.where(upper == 1, theirs, mine)
            back_s[:GROUP] = jnp.where(upper == 1, mine, theirs)

        @pl.when(v == CORR_STEP)
        def _():
            for k in range(1, halves):
                gather(k).wait()
            coef = coef_s[pl.ds(place * count, count), :]
            for n1 in range(0, half, 2):
                pair = [bg_s[pl.ds(n1 + j, MODES, stride=half), :] for j in range(2)]
                high, low = split(jnp.concatenate(pair, axis=1))
                fix = dot(coef, jnp.concatenate([high, low, high], axis=0))
                for j in range(2):
                    corr_s[pl.ds(n1 + j, count, stride=half), :] = fix[:, j * LANE : (j + 1) * LANE]

            def mend(i, carry):
                out_ref[i] = out_ref[i] + corr_s[pl.ds(i * half, half), :]
                return carry

            lax.fori_loop(0, (CORR_STEP - 1) * CHUNK, mend, 0)

        @pl.when(jnp.logical_not(is_mode))
        def _():
            receive(c)

        which = is_mode.astype(jnp.int32)
        front(which, zk_s)
        o = inverse(zk_s, bwd_s, fin_s, tw_s, uk_s)
        for i in range(CHUNK):
            res_s[i] = o[:, i * LANE : (i + 1) * LANE] + edges(which, i)

        @pl.when(is_mode)
        def _():
            for i in range(GROUP):
                order = jnp.bitwise_and(yy * GROUP + i, KMAX - 1)
                keep = jnp.where(order < cutoff_ref[0], 1.0, 0.0)
                bg_s[i * half : (i + 1) * half, :] = res_s[i] * keep
            for k in range(1, halves):
                gather(k).start()

        @pl.when(jnp.logical_and(jnp.logical_not(is_mode), v < CORR_STEP))
        def _():
            out_ref[pl.ds(c * CHUNK, CHUNK)] = res_s[...]

        @pl.when(v >= CORR_STEP)
        def _():
            rows = corr_s[pl.ds(c * CHUNK * half, CHUNK * half), :]
            out_ref[pl.ds(c * CHUNK, CHUNK)] = res_s[...] + rows.reshape(CHUNK, half, LANE)

        return carry

    lax.fori_loop(0, chunks, step, 0)
    for i in range(CHUNK):
        bias_o[i] = corr_s[((chunks - 1) * CHUNK + i) * half : ((chunks - 1) * CHUNK + i + 1) * half, :]
    receive(chunks - 1)
    front(0, zk_o)
    for i in range(CHUNK):
        bias_o[i] = bias_o[i] + edges(0, i)


def local(intensity, flat_field, dark_field, correlation, blend_width, padding, cutoff):
    angle_count = lax.axis_size("angle")
    total = intensity.shape[0]
    count = total // 2
    pixels = intensity.shape[2]
    length = 4 * pixels
    blocks = pixels // LANE
    half = LANE // 2
    tables = constants(length, angle_count, total)
    tables = [jnp.asarray(tables[name]) for name in NAMES]
    block = GROUP * blocks
    peers = angle_count // 2
    f32, bf16 = jnp.float32, jnp.bfloat16
    dma = pltpu.SemaphoreType.DMA
    scratch = [pltpu.VMEM(t.shape, t.dtype) for t in tables[: len(SCRATCH_NAMES)]] + [
        pltpu.VMEM((total * blocks, LANE), f32),
        pltpu.VMEM((count * blocks, LANE), f32),
        pltpu.VMEM((MODES * blocks, LANE), f32),
        pltpu.VMEM((peers, block, LANE), f32),
        pltpu.VMEM((block, LANE), f32),
        pltpu.VMEM((block, LANE), f32),
        pltpu.VMEM((MODES * half, LANE), f32),
        pltpu.VMEM((count * half, LANE), f32),
        pltpu.VMEM((4 * half, LANE), f32),
        pltpu.VMEM((LANE, 3 * STACK), bf16),
        pltpu.VMEM((CHUNK, blocks, LANE), f32),
        pltpu.VMEM((CHUNK, blocks, LANE), f32),
        pltpu.VMEM((CHUNK, STACK - blocks + 8, LANE), f32),
        pltpu.VMEM((3 * STACK, CHUNK * LANE), bf16),
        pltpu.VMEM((CHUNK * half, 6 * LANE), bf16),
        pltpu.VMEM((CHUNK * half, 6 * LANE), bf16),
        pltpu.VMEM((3 * LANE, CHUNK * LANE), bf16),
        pltpu.VMEM((CHUNK, half, LANE), f32),
        pltpu.VMEM((2, CHUNK, LANE), f32),
        dma((len(tables),)),
        dma,
        dma,
        dma,
        dma((count // CHUNK,)),
        dma((count // CHUNK,)),
        dma((peers,)),
        dma((peers,)),
        dma,
        dma,
        dma((peers,)),
        dma((peers,)),
        pltpu.VMEM((blocks, LANE), f32),
        pltpu.VMEM((blocks, LANE), f32),
    ]
    shape = jax.ShapeDtypeStruct
    outs = [
        shape((count - CHUNK, half, LANE), f32),
        shape((CHUNK * half, 6 * LANE), bf16),
        shape((CHUNK, half, LANE), f32),
    ] + [shape(tables[NAMES.index(name)].shape, tables[NAMES.index(name)].dtype) for name in ("backward", "final", "twiddle")]
    parts = pl.pallas_call(
        body_kernel,
        out_shape=outs,
        in_specs=[pl.BlockSpec(memory_space=pltpu.SMEM)] * 4
        + [pl.BlockSpec(memory_space=pltpu.HBM)] * (3 + len(tables)),
        out_specs=[pl.BlockSpec(memory_space=pltpu.VMEM)] * len(outs),
        scratch_shapes=scratch,
        compiler_params=pltpu.CompilerParams(
            vmem_limit_bytes=20 << 20, collective_id=0, has_side_effects=True
        ),
        name="filter_rows",
    )(
        correlation,
        blend_width,
        padding,
        cutoff,
        *[
            pltpu.with_memory_space_constraint(a, pltpu.HBM)
            for a in (
                intensity.reshape(total * blocks, LANE),
                flat_field.reshape(blocks, LANE),
                dark_field.reshape(blocks, LANE),
                *tables,
            )
        ],
    )
    out = pl.pallas_call(
        finish_kernel,
        out_shape=shape((count, half, LANE), f32),
        in_specs=[pl.BlockSpec(memory_space=pltpu.VMEM)] * len(parts),
        out_specs=pl.BlockSpec(memory_space=pltpu.HBM),
        scratch_shapes=[
            pltpu.VMEM((3 * LANE, CHUNK * LANE), bf16),
            pltpu.VMEM((CHUNK, half, LANE), f32),
            dma((count // CHUNK,)),
        ],
        compiler_params=pltpu.CompilerParams(vmem_limit_bytes=16 << 20),
        name="finish_rows",
    )(*parts)
    return out.reshape(count, 1, 2 * pixels)


def solution(mesh):
    placed = (P("angle", "row", None), P("row", None), P("row", None), P(), P(), P(), P())
    return jax.shard_map(
        local, mesh=mesh, in_specs=placed, out_specs=P("angle", "row", None), check_vma=False
    )
```

```python
import functools

import jax
import jax.numpy as jnp
import numpy as np
from jax import lax
from jax.experimental import pallas as pl
from jax.experimental.pallas import tpu as pltpu
from jax.sharding import PartitionSpec as P

KMAX = 8
FCUT = 512
OVL_LO = 512
OVL_HI = 1536
LANE = 128
MODES = 16
GROUP = 4
CHUNK = 8
STACK = 80
SUM_STEP = 1
MODE_STEP = 3
CORR_STEP = 5
FIRST = 3
MESH = pl.DeviceIdType.MESH


def split_np(table):
    high = table.astype(jnp.bfloat16)
    low = (table - high.astype(np.float64)).astype(jnp.bfloat16)
    return high, low


def split(value):
    high = value.astype(jnp.bfloat16)
    low = (value - high.astype(jnp.float32)).astype(jnp.bfloat16)
    return high, low


@functools.cache
def constants(length, angle_count, total):
    kept = length // 2
    freq = np.arange(kept, dtype=np.float64)
    ramp = freq / kept * (1.0 + np.cos(np.pi * freq / kept))
    drop = 1.0 - 1.0 / (1.0 + (freq / FCUT) ** 8)
    half = LANE // 2
    gains, sums = [], []
    reach = length * 3 // 4
    for gain in (ramp, ramp * drop):
        full = np.zeros(length)
        full[:kept] = gain
        full[kept + 1 :] = gain[:0:-1]
        kernel = np.fft.ifft(full).real
        offsets = np.arange(-reach, reach + 1)
        table = np.concatenate([[0.0], np.cumsum(kernel[offsets % length])])
        sums.append(np.pad(table, (0, -len(table) % LANE + LANE)).reshape(-1, LANE))
        place = np.arange(length)
        signed = np.where(place < kept, place, place - length)
        turned = kernel * np.exp(-1j * np.pi * signed / length)
        turned[kept] = 0.0
        between = np.fft.fft(turned).real
        k1 = np.arange(half)[:, None]
        k2 = np.arange(LANE)[None, :]
        gains.append(between[k1 + LANE * k2] * (2.0 / length))
    k1 = np.arange(half)[:, None]
    n2 = np.arange(LANE)[None, :]
    turn = 2.0 * np.pi * (k1 + 0.5) * n2 / length
    twiddle = np.stack([np.cos(turn), np.sin(turn)]).astype(np.float32)
    a = np.arange(LANE)[:, None]
    b = np.arange(LANE)[None, :]
    angle = 2.0 * np.pi * (a * b % LANE) / LANE
    c, s = np.cos(angle), np.sin(angle)
    high, low = split_np(np.block([[c, -s], [s, c]]))
    forward = np.concatenate([high, high, low], axis=0)
    high, low = split_np(np.block([[c, s], [-s, c]]))
    backward = np.concatenate([high, high, low], axis=0)
    n1 = np.arange(half)[:, None]
    last = 2.0 * np.pi * ((2 * np.arange(half)[None, :] + 1) * n1 % (2 * LANE)) / (2 * LANE)
    high, low = split_np(np.concatenate([np.cos(last), -np.sin(last)], axis=1))
    final = np.concatenate([high, high, low], axis=1)
    blocks = length // 4 // LANE
    firsts = []
    for q in range((length // 4 - OVL_HI) // LANE, (length // 4 - OVL_LO) // LANE + 1):
        index = np.concatenate([blocks - 1 - np.arange(blocks), q + np.arange(STACK - blocks)])[None, :]
        turn = np.pi * ((2 * k1 + 1) * index % (2 * LANE)) / LANE
        high, low = split_np(np.concatenate([np.cos(turn), -np.sin(turn)], axis=0))
        firsts.append(np.concatenate([high, high, low], axis=1))
    halves = angle_count // 2
    half_turn = angle_count * total // 2
    orders = np.arange(KMAX)[:, None]
    phis, coefs = [], []
    for place in range(angle_count):
        base = place % halves * total
        turn = 2.0 * np.pi * (orders * (base + np.arange(total)[None, :]) % half_turn) / half_turn
        table = np.concatenate([np.cos(turn), np.sin(turn)], axis=0)
        if place < halves:
            high, low = split_np(table)
            phis.append(np.concatenate([high, high, low], axis=1))
        start = place // halves * (total // 2)
        table = table[:, start : start + total // 2] * (-2.0 / half_turn)
        table[0] *= 0.5
        groups = table.reshape(halves, GROUP, -1)
        table = np.concatenate([groups[(place % halves - k) % halves] for k in range(halves)], axis=0)
        high, low = split_np(table.T)
        coefs.append(np.concatenate([high, high, low], axis=1))
    return dict(
        phi=np.concatenate(phis, axis=0),
        first=np.concatenate(firsts, axis=0),
        sums=np.concatenate(sums, axis=0).astype(np.float32),
        gain=np.concatenate(gains, axis=0).astype(np.float32),
        twiddle=twiddle.reshape(2 * half, LANE),
        forward=forward,
        backward=backward,
        final=final,
        coef=np.concatenate(coefs, axis=0),
    )


def dot(a, b):
    return jnp.dot(a, b, preferred_element_type=jnp.float32)


def cut(sums_s, which, start):
    half = LANE // 2
    rows = sums_s.shape[0] // 2
    row = lax.shift_right_logical(start, 7)
    rest = jnp.bitwise_and(start, LANE - 1)
    back = jnp.bitwise_and(LANE - rest, LANE - 1)
    here = pltpu.roll(sums_s[pl.ds(which * rows + row, half), :], back, 1)
    there = pltpu.roll(sums_s[pl.ds(which * rows + row + 1, half), :], back, 1)
    lane = lax.broadcasted_iota(jnp.int32, (half, LANE), 1)
    return jnp.where(lane < LANE - rest, here, there)


SCRATCH_NAMES = ("phi", "first", "sums", "gain", "forward", "coef")
NAMES = SCRATCH_NAMES + ("twiddle", "backward", "final")


def inverse(zk_s, bwd_s, fin_s, tw_s, uk_s, size=CHUNK):
    half = LANE // 2
    u = dot(zk_s[: size * half, :], bwd_s[...])
    cos, sin = tw_s[:half, :], tw_s[half:, :]
    for i in range(size):
        re = u[i * half : (i + 1) * half, :LANE]
        im = u[i * half : (i + 1) * half, LANE:]
        high, low = split(jnp.concatenate([re * cos - im * sin, im * cos + re * sin], axis=0))
        cols = slice(i * LANE, (i + 1) * LANE)
        uk_s[:LANE, cols] = high
        uk_s[LANE : 2 * LANE, cols] = low
        uk_s[2 * LANE :, cols] = high
    return dot(fin_s[...], uk_s[:, : size * LANE])


def finish_kernel(out_ref, zk_ref, bias_ref, bwd_ref, fin_ref, tw_ref, y_ref, uk_s, res_s, sems):
    done = out_ref.shape[0]
    part = done // (sems.shape[0] - 1)
    copies = [
        pltpu.make_async_copy(
            out_ref.at[pl.ds(i * part, part)], y_ref.at[pl.ds(i * part, part)], sems.at[i]
        )
        for i in range(done // part)
    ]
    for copy in copies:
        copy.start()
    o = inverse(zk_ref, bwd_ref, fin_ref, tw_ref, uk_s)
    for i in range(CHUNK):
        res_s[i] = o[:, i * LANE : (i + 1) * LANE] + bias_ref[i]
    last = pltpu.make_async_copy(res_s, y_ref.at[pl.ds(done, CHUNK)], sems.at[done // part])
    last.start()
    for copy in copies:
        copy.wait()
    last.wait()


def body_kernel(*refs):
    scalar_refs, (x_ref, flat_ref, dark_ref) = refs[:4], refs[4:7]
    tables = refs[7 : 7 + len(NAMES)]
    out_ref, zk_o, bias_o, bwd_s, fin_s, tw_s = refs[7 + len(NAMES) : 13 + len(NAMES)]
    rest = refs[13 + len(NAMES) :]
    (xs, got_s, gown_s, rs_s, sum_s, gx_s, bg_s, corr_s, edge_t, first_d,
     main_s, back_s, shift_s, xk_s, yk_s, zk_s, uk_s, edge_s,
     tsem, xsem, fsem, dsem, ex_send, ex_recv, rs_send, rs_recv, gx_send, gx_recv, ag_send, ag_recv,
     flat_s, dark_s) = rest[len(SCRATCH_NAMES) :]
    phi_s, first_s, sums_s, gain_s, fwd_s, coef_s = rest[: len(SCRATCH_NAMES)]
    held = (phi_s, first_s, sums_s, gain_s, fwd_s, coef_s, tw_s, bwd_s, fin_s)

    place = lax.axis_index("angle")
    row = lax.axis_index("row")
    halves = GROUP
    yy = lax.rem(place, halves)
    upper = place // halves
    half = LANE // 2
    wide = 2 * LANE
    blocks = flat_ref.shape[0]
    total = xs.shape[0] // blocks
    count = total // 2
    chunks = count // CHUNK
    length = 4 * blocks * LANE
    kept = length // 2
    reach = length * 3 // 4
    partner = (lax.rem(place + halves, 2 * halves), row)
    peers = [(upper * halves + lax.rem(yy + k, halves), row) for k in range(halves)]

    barrier = pltpu.get_barrier_semaphore()
    pl.semaphore_signal(barrier, inc=1, device_id=partner, device_id_type=MESH)
    for k in range(1, halves):
        pl.semaphore_signal(barrier, inc=1, device_id=peers[k], device_id_type=MESH)
    load_x = pltpu.make_async_copy(x_ref, xs, xsem)
    load_x.start()
    load_f = pltpu.make_async_copy(flat_ref, flat_s, fsem)
    load_f.start()
    load_d = pltpu.make_async_copy(dark_ref, dark_s, dsem)
    load_d.start()
    loads = [pltpu.make_async_copy(tables[i], held[i], tsem.at[i]) for i in range(len(NAMES))]
    loads[0].start()
    corr_ref, blend_ref, pad_ref, cutoff_ref = scalar_refs
    pl.semaphore_wait(barrier, halves)

    span = CHUNK * blocks

    def exchange(c):
        return pltpu.make_async_remote_copy(
            src_ref=x_ref.at[pl.ds((1 - upper) * count * blocks + c * span, span), :],
            dst_ref=got_s.at[pl.ds(c * span, span), :],
            send_sem=ex_send.at[c],
            recv_sem=ex_recv.at[c],
            device_id=partner,
            device_id_type=MESH,
        )

    for c in range(FIRST):
        exchange(c).start()
    for load in loads[1:]:
        load.start()

    block = GROUP * blocks

    def scatter(k):
        return pltpu.make_async_remote_copy(
            src_ref=gown_s.at[pl.ds(lax.rem(yy + k, halves) * block, block), :],
            dst_ref=rs_s.at[k],
            send_sem=rs_send.at[k],
            recv_sem=rs_recv.at[k],
            device_id=peers[k],
            device_id_type=MESH,
        )

    def across():
        return pltpu.make_async_remote_copy(
            src_ref=sum_s,
            dst_ref=gx_s,
            send_sem=gx_send,
            recv_sem=gx_recv,
            device_id=partner,
            device_id_type=MESH,
        )

    def gather(k):
        return pltpu.make_async_remote_copy(
            src_ref=bg_s.at[pl.ds(0, GROUP * half), :],
            dst_ref=bg_s.at[pl.ds(k * GROUP * half, GROUP * half), :],
            send_sem=ag_send.at[k],
            recv_sem=ag_recv.at[k],
            device_id=peers[k],
            device_id_type=MESH,
        )

    load_f.wait()
    load_d.wait()
    load_x.wait()
    loads[0].wait()

    phi = phi_s[pl.ds(yy * MODES, MODES), :]
    for n1 in range(blocks):
        dark = dark_s[n1 : n1 + 1, :]
        base = jnp.log(flat_s[n1 : n1 + 1, :] - dark)
        rows = xs[pl.ds(n1, total, stride=blocks), :]
        high, low = split(base - jnp.log(rows - dark))
        gown_s[pl.ds(n1, MODES, stride=blocks), :] = dot(phi, jnp.concatenate([high, low, high], axis=0))
    for k in range(1, halves):
        scatter(k).start()

    for load in loads[1:]:
        load.wait()
    corr = corr_ref[0]
    pad = pad_ref[0]
    blend = blend_ref[0].astype(jnp.float32)
    shift = blocks * LANE - corr
    q = lax.shift_right_logical(shift, 7)
    roll_by = jnp.bitwise_and(shift, LANE - 1)
    least = blocks - OVL_HI // LANE
    q = jnp.clip(q - least, 0, first_s.shape[0] // LANE - 1)
    first_d[...] = first_s[pl.ds(q * LANE, LANE), :]
    for which in range(2):
        tail = cut(sums_s, which, 1 - kept + corr + reach) - cut(sums_s, which, 1 - kept - pad + reach)
        ahead = cut(sums_s, which, 1 + pad + reach) - cut(sums_s, which, jnp.int32(1 + reach))
        edge_t[which * LANE : which * LANE + half, :] = tail
        edge_t[which * LANE + half : (which + 1) * LANE, :] = ahead
    shift_s[...] = jnp.zeros_like(shift_s)
    pixel = (
        lax.broadcasted_iota(jnp.int32, (blocks, LANE), 0) * LANE
        + lax.broadcasted_iota(jnp.int32, (blocks, LANE), 1)
    ).astype(jnp.float32)

    def receive(c):
        dark = dark_s[...]
        base = jnp.log(flat_s[...] - dark)
        own = xs[pl.ds(upper * count * blocks + c * span, span), :].reshape(CHUNK, blocks, LANE)
        own = base - jnp.log(own - dark)
        exchange(c).wait()
        got = base - jnp.log(got_s[pl.ds(c * span, span), :].reshape(CHUNK, blocks, LANE) - dark)
        main_s[...] = jnp.where(upper == 1, got, own)
        back_s[...] = jnp.where(upper == 1, own, got)

    def front(which, zk_s, size=CHUNK):
        weight = jnp.clip((pixel + 0.5 - corr.astype(jnp.float32) * 0.5) / blend + 0.5, 0.0, 1.0)
        lanes = lax.broadcasted_iota(jnp.int32, (blocks, LANE), 1)
        lanes48 = lax.broadcasted_iota(jnp.int32, (STACK - blocks, LANE), 1)
        for i in range(size):
            main = main_s[i]
            back = back_s[i]
            edge_s[0, i : i + 1, :] = jnp.broadcast_to(main[blocks - 1 : blocks, LANE - 1 :], (1, LANE))
            edge_s[1, i : i + 1, :] = jnp.broadcast_to(back[blocks - 1 : blocks, LANE - 1 :], (1, LANE))
            left = jnp.take_along_axis(back * weight, LANE - 1 - lanes, axis=1)
            shift_s[i, 8 : 8 + blocks, :] = pltpu.roll(main * weight, roll_by, 1)
            here = shift_s[i, 8 : 8 + STACK - blocks, :]
            prev = shift_s[i, 7 : 7 + STACK - blocks, :]
            right = jnp.where(lanes48 >= roll_by, here, prev)
            high, low = split(jnp.concatenate([left, right], axis=0))
            cols = slice(i * LANE, (i + 1) * LANE)
            xk_s[:STACK, cols] = high
            xk_s[STACK : 2 * STACK, cols] = low
            xk_s[2 * STACK :, cols] = high
        y = dot(first_d[...], xk_s[:, : size * LANE])
        cos, sin = tw_s[:half, :], tw_s[half:, :]
        for i in range(size):
            re = y[:half, i * LANE : (i + 1) * LANE]
            im = y[half:, i * LANE : (i + 1) * LANE]
            high, low = split(jnp.concatenate([re * cos + im * sin, im * cos - re * sin], axis=1))
            rows = slice(i * half, (i + 1) * half)
            yk_s[rows, :wide] = high
            yk_s[rows, wide : 2 * wide] = low
            yk_s[rows, 2 * wide :] = high
        gain = gain_s[which * half : (which + 1) * half, :]
        gain2 = jnp.concatenate([gain, gain], axis=1)
        z = dot(yk_s[: size * half, :], fwd_s[...])
        for i in range(size):
            rows = slice(i * half, (i + 1) * half)
            high, low = split(z[rows] * gain2)
            zk_s[rows, :wide] = high
            zk_s[rows, wide : 2 * wide] = low
            zk_s[rows, 2 * wide :] = high

    def edges(which, i):
        tail = edge_t[which * LANE : which * LANE + half, :]
        ahead = edge_t[which * LANE + half : (which + 1) * LANE, :]
        return edge_s[0, i : i + 1, :] * tail + edge_s[1, i : i + 1, :] * ahead

    def mode_sums():
        for k in range(1, halves):
            scatter(k).wait()
        sum_s[...] = gown_s[pl.ds(yy * block, block), :] + rs_s[1] + rs_s[2] + rs_s[3]
        across().start()
        for c in range(FIRST, chunks):
            exchange(c).start()

    def data_step(c, corrected):
        receive(c)
        front(0, zk_s)
        o = inverse(zk_s, bwd_s, fin_s, tw_s, uk_s)
        for i in range(CHUNK):
            line = o[:, i * LANE : (i + 1) * LANE] + edges(0, i)
            if corrected:
                line = line + corr_s[pl.ds((c * CHUNK + i) * half, half), :]
            out_ref[c * CHUNK + i] = line

    def early(c, carry):
        @pl.when(c == SUM_STEP)
        def _():
            mode_sums()

        data_step(c, False)
        return carry

    def middle(c, carry):
        data_step(c, False)
        return carry

    def late(c, carry):
        data_step(c, True)
        return carry

    lax.fori_loop(0, MODE_STEP, early, 0)

    across().wait()
    mine = sum_s[...].reshape(GROUP, blocks, LANE)
    theirs = gx_s[...].reshape(GROUP, blocks, LANE)
    main_s[:GROUP] = jnp.where(upper == 1, theirs, mine)
    back_s[:GROUP] = jnp.where(upper == 1, mine, theirs)
    front(1, zk_s, GROUP)
    o = inverse(zk_s, bwd_s, fin_s, tw_s, uk_s, GROUP)
    for i in range(GROUP):
        order = jnp.bitwise_and(yy * GROUP + i, KMAX - 1)
        keep = jnp.where(order < cutoff_ref[0], 1.0, 0.0)
        bg_s[i * half : (i + 1) * half, :] = (o[:, i * LANE : (i + 1) * LANE] + edges(1, i)) * keep
    for k in range(1, halves):
        gather(k).start()

    lax.fori_loop(MODE_STEP, CORR_STEP, middle, 0)

    for k in range(1, halves):
        gather(k).wait()
    coef = coef_s[pl.ds(place * count, count), :]
    for n1 in range(0, half, 2):
        pair = [bg_s[pl.ds(n1 + j, MODES, stride=half), :] for j in range(2)]
        high, low = split(jnp.concatenate(pair, axis=1))
        fix = dot(coef, jnp.concatenate([high, low, high], axis=0))
        for j in range(2):
            corr_s[pl.ds(n1 + j, count, stride=half), :] = fix[:, j * LANE : (j + 1) * LANE]

    def mend(i, carry):
        out_ref[i] = out_ref[i] + corr_s[pl.ds(i * half, half), :]
        return carry

    lax.fori_loop(0, CORR_STEP * CHUNK, mend, 0)
    lax.fori_loop(CORR_STEP, chunks - 1, late, 0)
    for i in range(CHUNK):
        bias_o[i] = corr_s[((chunks - 1) * CHUNK + i) * half : ((chunks - 1) * CHUNK + i + 1) * half, :]
    receive(chunks - 1)
    front(0, zk_o)
    for i in range(CHUNK):
        bias_o[i] = bias_o[i] + edges(0, i)


def local(intensity, flat_field, dark_field, correlation, blend_width, padding, cutoff):
    angle_count = lax.axis_size("angle")
    total = intensity.shape[0]
    count = total // 2
    pixels = intensity.shape[2]
    length = 4 * pixels
    blocks = pixels // LANE
    half = LANE // 2
    tables = constants(length, angle_count, total)
    tables = [jnp.asarray(tables[name]) for name in NAMES]
    block = GROUP * blocks
    peers = angle_count // 2
    f32, bf16 = jnp.float32, jnp.bfloat16
    dma = pltpu.SemaphoreType.DMA
    scratch = [pltpu.VMEM(t.shape, t.dtype) for t in tables[: len(SCRATCH_NAMES)]] + [
        pltpu.VMEM((total * blocks, LANE), f32),
        pltpu.VMEM((count * blocks, LANE), f32),
        pltpu.VMEM((MODES * blocks, LANE), f32),
        pltpu.VMEM((peers, block, LANE), f32),
        pltpu.VMEM((block, LANE), f32),
        pltpu.VMEM((block, LANE), f32),
        pltpu.VMEM((MODES * half, LANE), f32),
        pltpu.VMEM((count * half, LANE), f32),
        pltpu.VMEM((4 * half, LANE), f32),
        pltpu.VMEM((LANE, 3 * STACK), bf16),
        pltpu.VMEM((CHUNK, blocks, LANE), f32),
        pltpu.VMEM((CHUNK, blocks, LANE), f32),
        pltpu.VMEM((CHUNK, STACK - blocks + 8, LANE), f32),
        pltpu.VMEM((3 * STACK, CHUNK * LANE), bf16),
        pltpu.VMEM((CHUNK * half, 6 * LANE), bf16),
        pltpu.VMEM((CHUNK * half, 6 * LANE), bf16),
        pltpu.VMEM((3 * LANE, CHUNK * LANE), bf16),
        pltpu.VMEM((2, CHUNK, LANE), f32),
        dma((len(tables),)),
        dma,
        dma,
        dma,
        dma((count // CHUNK,)),
        dma((count // CHUNK,)),
        dma((peers,)),
        dma((peers,)),
        dma,
        dma,
        dma((peers,)),
        dma((peers,)),
        pltpu.VMEM((blocks, LANE), f32),
        pltpu.VMEM((blocks, LANE), f32),
    ]
    shape = jax.ShapeDtypeStruct
    outs = [
        shape((count - CHUNK, half, LANE), f32),
        shape((CHUNK * half, 6 * LANE), bf16),
        shape((CHUNK, half, LANE), f32),
    ] + [shape(tables[NAMES.index(name)].shape, tables[NAMES.index(name)].dtype) for name in ("backward", "final", "twiddle")]
    parts = pl.pallas_call(
        body_kernel,
        out_shape=outs,
        in_specs=[pl.BlockSpec(memory_space=pltpu.SMEM)] * 4
        + [pl.BlockSpec(memory_space=pltpu.HBM)] * (3 + len(tables)),
        out_specs=[pl.BlockSpec(memory_space=pltpu.VMEM)] * len(outs),
        scratch_shapes=scratch,
        compiler_params=pltpu.CompilerParams(
            vmem_limit_bytes=20 << 20, collective_id=0, has_side_effects=True
        ),
        name="filter_rows",
    )(
        correlation,
        blend_width,
        padding,
        cutoff,
        *[
            pltpu.with_memory_space_constraint(a, pltpu.HBM)
            for a in (
                intensity.reshape(total * blocks, LANE),
                flat_field.reshape(blocks, LANE),
                dark_field.reshape(blocks, LANE),
                *tables,
            )
        ],
    )
    out = pl.pallas_call(
        finish_kernel,
        out_shape=shape((count, half, LANE), f32),
        in_specs=[pl.BlockSpec(memory_space=pltpu.VMEM)] * len(parts),
        out_specs=pl.BlockSpec(memory_space=pltpu.HBM),
        scratch_shapes=[
            pltpu.VMEM((3 * LANE, CHUNK * LANE), bf16),
            pltpu.VMEM((CHUNK, half, LANE), f32),
            dma((count // CHUNK,)),
        ],
        compiler_params=pltpu.CompilerParams(vmem_limit_bytes=16 << 20),
        name="finish_rows",
    )(*parts)
    return out.reshape(count, 1, 2 * pixels)


def solution(mesh):
    placed = (P("angle", "row", None), P("row", None), P("row", None), P(), P(), P(), P())
    return jax.shard_map(
        local, mesh=mesh, in_specs=placed, out_specs=P("angle", "row", None), check_vma=False
    )
```
